1024 devices in a mesh: dp: 64 (over y, x, core), tensor: 16 (over z).
Axes of the slice: x: 4, y: 8, z: 16, core: 2. Of those that a mesh axis runs over, the one named last changes fastest.
Arguments:
- layer_input: bfloat16 [32768, 8192], P('dp', 'tensor'), may hold values from -180 to 180
- gain: bfloat16 [8192], P('tensor'), may hold values from 0.25 to 1.75
- w_kv: bfloat16 [2048, 8192], P(None, 'tensor'), may hold values from -0.125 to 0.125
- d_kv: bfloat16 [32768, 2048], P('dp', 'tensor'), may hold values from -32 to 32
- destination: int32 [32768], P('dp'), may hold values from -1 to 63, as said below
Outputs:
- grad_x: bfloat16 [32768, 8192], P('dp', 'tensor')
- grad_weight: float32 [2048, 8192], P('dp', 'tensor')
The draws below stay inside these ranges and needn't reach their ends.
Inputs may be any that keep to these rules, and one draw needn't show every extreme that they name: The rows of one device with destination >= 0 are its first rows, 128 of them or more, and some device has no padding. At most 8 rows of one device name the same destination, and some destination is named by exactly 8 rows of every device.
All inputs are finite; a program needn't handle non-finite values.
Results may differ from the reference program's by a relative error of at most 0.0031.
Values may be sent and summed in bfloat16 or wider, within the bound.
No kernel may reach another device: no remote copies, remote signals or barrier semaphores. Data moves between devices by JAX's collectives and lax.ppermute only.
A program may use at most 32 MiB of HBM per device.

```python
import jax
import jax.numpy as jnp
from jax import lax

D = 8192
TOK_DEV = 512
KVW = 1024
ROWS_PEER = 8
TOKENS = 32768
N_DP = 64


def draw_layer_input(key, part):
    key_a, key_b, key_c = jax.random.split(jax.random.fold_in(key, 11), 3)
    column = jnp.arange(D, dtype=jnp.float32) / D
    column_scale = jnp.exp(jnp.log(3.0) * column) * jnp.exp(jnp.log(10.0) * jax.random.uniform(key_a, (D,), jnp.float32))
    row_scale = jnp.exp(jnp.log(10.0) * jax.random.uniform(key_b, (TOKENS, 1), jnp.float32))
    noise = jnp.clip(jax.random.normal(key_c, (TOKENS, D), jnp.float32), -6.0, 6.0)
    return (noise * column_scale * row_scale / 10.0).astype(jnp.bfloat16)


def draw_destination(key, part):
    base_key = jax.random.fold_in(key, 23)
    key_len, key_full, key_star, key_rows = jax.random.split(base_key, 4)
    lengths = jax.random.randint(key_len, (N_DP,), TOK_DEV // 4, TOK_DEV + 1)
    full_dev = jax.random.randint(key_full, (), 0, N_DP)
    lengths = jnp.where(jnp.arange(N_DP) == full_dev, TOK_DEV, lengths)
    star_dev = jax.random.randint(key_star, (), 0, N_DP)
    slot_dest = jnp.arange(TOK_DEV, dtype=jnp.int32) // ROWS_PEER
    row_ids = jnp.arange(TOK_DEV, dtype=jnp.int32)

    def one_device(device_key, length):
        key_order, key_shuffle = jax.random.split(device_key)
        order_perm = jax.random.permutation(key_order, TOK_DEV).astype(jnp.int32)
        priority = jnp.where(slot_dest == star_dev, 0, TOK_DEV) + order_perm
        chosen = jnp.argsort(priority)
        shuffle = jax.random.permutation(key_shuffle, TOK_DEV).astype(jnp.int32)
        is_live = row_ids < length
        below = (shuffle[None, :] < shuffle[:, None]) & is_live[None, :]
        live_rank = jnp.sum(below.astype(jnp.int32), axis=1)
        picked = chosen[jnp.minimum(live_rank, TOK_DEV - 1)]
        return jnp.where(is_live, slot_dest[picked], -1)
    dev_keys = jax.random.split(key_rows, N_DP)
    return jax.vmap(one_device)(dev_keys, lengths).reshape(TOKENS).astype(jnp.int32)


def spiked(entries, key, source, target, blocks, factor):
    def block_of(dim):
        return (jnp.arange(entries.shape[dim]) // (entries.shape[dim] // blocks)).reshape((-1,) + (1,) * (entries.ndim - 1 - dim))

    near = jax.random.permutation(key, blocks)[block_of(target)]
    second = (block_of(target) + blocks // 2) % blocks
    return jnp.where((block_of(source) == near) | (block_of(source) == second), factor * entries, entries)


def levels(rng, extent, pieces, least, largest):
    factor_of, own = 1.0, jax.random.fold_in(rng, 6)
    for axis_at, blocks in pieces:
        heights = jnp.exp(jax.random.uniform(jax.random.fold_in(own, axis_at), (blocks,), jnp.float32, least / len(pieces), largest / len(pieces)))
        factor_of = factor_of * jnp.repeat(heights, extent[axis_at] // blocks).reshape([-1 if axis == axis_at else 1 for axis in range(len(extent))])
    return factor_of


def gaussian(stream_key, extent, width, most, pieces=(), kind=jnp.bfloat16):
    array = jax.random.normal(stream_key, extent, jnp.float32) * width
    if len(pieces) > 0:
        array = levels(stream_key, extent, pieces, -0.22, 0.18) * array
    return jnp.clip(array, min=-most, max=most).astype(kind)


def gaussian_with(stream_key, dims, spread, most, shards, heavy, kind=jnp.bfloat16):
    array = spread * jax.random.normal(stream_key, dims, jnp.float32)
    if shards:
        array = array * levels(stream_key, dims, shards, -0.22, 0.18)
    return jnp.clip(spiked(array, jax.random.fold_in(stream_key, 3), *heavy), -most, most).astype(kind)


def setup_inputs(seed: int = 0) -> dict:
    streams_of = jax.random.split(jax.random.key(seed), 6)
    layer_input = draw_layer_input(jax.random.fold_in(streams_of[5], 71), 0)
    gain = jnp.clip(1.0 + 0.15 * jax.random.normal(streams_of[1], (D,), jnp.float32), 0.25, 1.75).astype(jnp.bfloat16)
    w_kv = gaussian(streams_of[2], (2 * KVW, D), (2 * KVW) ** -0.5, 0.125, ((1, 16),))
    d_kv = gaussian_with(streams_of[3], (TOKENS, 2 * KVW), 2.0, 32.0, ((0, 64), (1, 16)), (0, 1, 64, 4.0))
    destination = draw_destination(jax.random.fold_in(streams_of[5], 71), 0)
    return {"layer_input": layer_input, "gain": gain, "w_kv": w_kv, "d_kv": d_kv, "destination": destination}


EPS = 1e-06

def reference(layer_input, gain, w_kv, d_kv, destination):
    peer_ids = jnp.arange(N_DP, dtype=jnp.int32)
    gain_wide = gain.astype(jnp.float32)

    def owner_block(weight_acc, owner_idx):
        block_rows = lax.dynamic_slice_in_dim(layer_input, owner_idx * TOK_DEV, TOK_DEV, 0)
        target = lax.dynamic_slice_in_dim(destination, owner_idx * TOK_DEV, TOK_DEV, 0)
        onehot = (target[:, None] == peer_ids[None, :]).astype(jnp.int32)
        before = jnp.cumsum(onehot, axis=0) - onehot
        slot_rank = lax.optimization_barrier(jnp.sum(before * onehot, axis=1))
        is_live = target >= 0
        slot_index = jnp.where(is_live, target * TOK_DEV + owner_idx * ROWS_PEER + slot_rank, 0).astype(jnp.int32)
        cotangent = jnp.where(is_live[:, None], d_kv[slot_index], jnp.zeros((), d_kv.dtype))
        values = block_rows.astype(jnp.float32)
        inverse = lax.rsqrt(lax.optimization_barrier(jnp.mean(values * values, axis=1)) + EPS)
        normed = (values * inverse[:, None] * gain_wide).astype(jnp.bfloat16)
        dnormed = jnp.dot(cotangent, w_kv, preferred_element_type=jnp.float32)
        mean_dot = lax.optimization_barrier(jnp.mean(values * gain_wide * dnormed, axis=1))
        grad_rows = (inverse[:, None] * gain_wide * dnormed - values * (inverse ** 3 * mean_dot)[:, None]).astype(jnp.bfloat16)
        term = lax.dot_general(cotangent, normed, (((0,), (0,)), ((), ())), preferred_element_type=jnp.float32)
        return (weight_acc + term, grad_rows)
    weight, grads = lax.scan(owner_block, jnp.zeros((2 * KVW, D), jnp.float32), jnp.arange(N_DP, dtype=jnp.int32))
    return (grads.reshape(TOKENS, D), weight)
```

```python
import jax
import jax.numpy as jnp
from jax import lax
from jax.experimental import pallas as pl
from jax.experimental.pallas import tpu as pltpu
from jax.sharding import Mesh, PartitionSpec as P

D = 8192
EPS = 1e-06
ROWS = 512
FEAT = 512
COLS = 128
TP = 16
CHIPS = 32
PAD = 16
BLOCK = COLS + PAD


def place_kernel(received, onehot, stats, out):
    picked = lax.dot_general(
        received[...], onehot[...], (((0,), (0,)), ((), ())), preferred_element_type=jnp.float32
    )
    out[:COLS, :] = picked.astype(jnp.bfloat16)
    out[COLS:, :] = stats[...]


def place(received, onehot, stats):
    return pl.pallas_call(
        place_kernel,
        out_shape=jax.ShapeDtypeStruct((BLOCK, ROWS), jnp.bfloat16),
        name="place",
    )(received, onehot, stats)


def core_kernel(position, *refs):
    blocks = refs[:TP]
    w, x, gain, keep, send, dnormed, inverse, products = refs[TP:]
    me, core = position[0], position[1]
    total = jnp.zeros((1, ROWS), jnp.float32)
    for block in blocks:
        rows = block[COLS:, :].astype(jnp.float32)
        total = total + (rows[0:1] + rows[1:2] + rows[2:3])
    inv = lax.rsqrt(total / D + EPS)
    inverse[...] = inv
    column = jnp.broadcast_to(inv, (COLS, ROWS)).T
    values = x[...].astype(jnp.float32)
    gain_wide = gain[...].astype(jnp.float32)
    normed = (values * jnp.concatenate([column] * (FEAT // COLS), axis=1) * gain_wide).astype(jnp.bfloat16)
    first = core == 0
    grad = jnp.zeros((ROWS, FEAT), jnp.float32)
    for step, block in enumerate(blocks):
        owner = lax.rem(me + step, TP)
        cot = block[:COLS, :]
        rows = w[pl.ds(pl.multiple_of(owner * COLS, COLS), COLS), :]
        grad = grad + lax.dot_general(
            cot, rows, (((0,), (0,)), ((), ())), preferred_element_type=jnp.float32
        )
        term = jnp.dot(cot, normed, preferred_element_type=jnp.float32)
        at = pl.multiple_of(owner * (COLS // 2), COLS // 2)
        for half in range(2):
            low = term[64 * half : 64 * half + 32]
            high = term[64 * half + 32 : 64 * half + 64]
            keep[pl.ds(at + 32 * half, 32), :] = jnp.where(first, low, high)
            send[pl.ds(at + 32 * half, 32), :] = jnp.where(first, high, low).astype(jnp.bfloat16)
    dnormed[...] = grad
    part = values * gain_wide * grad
    lanes = part[:, :COLS]
    for i in range(1, FEAT // COLS):
        lanes = lanes + part[:, COLS * i : COLS * (i + 1)]
    products[...] = jnp.sum(lanes.T, axis=0, keepdims=True)


def core_step(position, blocks, w_kv, x, gain):
    half = 2 * D // 16
    return pl.pallas_call(
        core_kernel,
        in_specs=[pl.BlockSpec(memory_space=pltpu.SMEM)] + [pl.BlockSpec(memory_space=pltpu.VMEM)] * (TP + 3),
        out_specs=[pl.BlockSpec(memory_space=pltpu.VMEM)] * 5,
        out_shape=[
            jax.ShapeDtypeStruct((half, FEAT), jnp.float32),
            jax.ShapeDtypeStruct((half, FEAT), jnp.bfloat16),
            jax.ShapeDtypeStruct((ROWS, FEAT), jnp.float32),
            jax.ShapeDtypeStruct((1, ROWS), jnp.float32),
            jax.ShapeDtypeStruct((1, ROWS), jnp.float32),
        ],
        compiler_params=pltpu.CompilerParams(vmem_limit_bytes=40 * 1024 * 1024),
        name="core_step",
    )(position, *blocks, w_kv, x, gain)


def shards(layer_input, gain, w_kv, d_kv, destination):
    me = lax.axis_index("tensor")
    core = lax.axis_index("core")
    right = [(i, (i + 1) % TP) for i in range(TP)]
    left = [(i, (i - 1) % TP) for i in range(TP)]

    received = lax.all_to_all(d_kv, ("chip", "core"), split_axis=0, concat_axis=0, tiled=True)

    ids = jnp.arange(ROWS, dtype=jnp.int32)
    same = (destination[:, None] == destination[None, :]) & (ids[:, None] < ids[None, :])
    slot_rank = jnp.sum(same.astype(jnp.int32), axis=0)
    is_live = destination >= 0
    position = jnp.where(is_live, destination * 8 + slot_rank, -1)
    onehot = (ids[:, None] == position[None, :]).astype(jnp.bfloat16)

    values = layer_input.astype(jnp.float32)
    squares = jnp.sum(values * values, axis=1)
    top = lax.reduce_precision(squares, 8, 7)
    rest = squares - top
    middle = lax.reduce_precision(rest, 8, 7)
    stats = jnp.stack([top, middle, rest - middle]).astype(jnp.bfloat16)
    stats = jnp.concatenate([stats, jnp.zeros((PAD - 3, ROWS), jnp.bfloat16)], axis=0)

    own = place(received, onehot, stats)
    blocks = [None] * TP
    blocks[0] = ahead = behind = own
    for step in range(1, TP // 2 + 1):
        behind = lax.ppermute(behind, "tensor", right)
        blocks[TP - step] = behind
        if step < TP // 2:
            ahead = lax.ppermute(ahead, "tensor", left)
            blocks[step] = ahead

    where = jnp.stack([me, core]).astype(jnp.int32)
    keep, send, dnormed, inverse, products = core_step(where, blocks, w_kv, layer_input, gain[None, :])

    taken = lax.ppermute(send, "core", [(0, 1), (1, 0)])
    pair = (keep + taken.astype(jnp.float32)).astype(jnp.bfloat16)
    parts = lax.all_to_all(pair, "chip", split_axis=0, concat_axis=0, tiled=True)
    grad_weight = jnp.sum(parts.reshape(CHIPS, 32, FEAT).astype(jnp.float32), axis=0)

    spread = lax.all_to_all(
        jnp.broadcast_to(products, (TP, ROWS)), "tensor", split_axis=0, concat_axis=0, tiled=True
    )
    mean_dot = jnp.sum(spread, axis=0) / D
    inv = inverse[0]
    gain_wide = gain.astype(jnp.float32)
    grad_x = (inv[:, None] * gain_wide * dnormed - values * (inv**3 * mean_dot)[:, None]).astype(jnp.bfloat16)
    return (grad_x, grad_weight)


def solution(mesh):
    fine = Mesh(mesh.devices.reshape(CHIPS, 2, TP), ("chip", "core", "tensor"))
    dp = ("chip", "core")
    return jax.shard_map(
        shards,
        mesh=fine,
        in_specs=(P(dp, "tensor"), P("tensor"), P(None, "tensor"), P(dp, "tensor"), P(dp)),
        out_specs=(P(dp, "tensor"), P(dp, "tensor")),
        check_vma=False,
    )
```

```python
import jax
import jax.numpy as jnp
from jax import lax
from jax.experimental import pallas as pl
from jax.experimental.pallas import tpu as pltpu
from jax.sharding import Mesh, PartitionSpec as P

D = 8192
EPS = 1e-06
ROWS = 512
FEAT = 512
COLS = 128
FAR = 4
NEAR = 4
TP = FAR * NEAR
CHIPS = 32
DP = 2 * CHIPS
HALF = FAR * COLS // 2
KV = TP * COLS
Z = ("zh", "zl")


def place_kernel(received, onehot, out):
    for i in range(FAR):
        picked = lax.dot_general(
            received[ROWS * i : ROWS * (i + 1), :],
            onehot[...],
            (((0,), (0,)), ((), ())),
            preferred_element_type=jnp.float32,
        )
        out[COLS * i : COLS * (i + 1), :] = picked.astype(jnp.bfloat16)


def place(received, onehot):
    return pl.pallas_call(
        place_kernel,
        out_shape=jax.ShapeDtypeStruct((FAR * COLS, ROWS), jnp.bfloat16),
        name="place",
    )(received, onehot)


def core_kernel(position, own, right, left, far_a, far_b, w, x, gain, normed, keep, send, dnormed, products, cot, weights, grad, sems):
    near, core = position[0], position[1]
    load_w = pltpu.make_async_copy(w, weights, sems.at[0])
    load_w.start()
    loads = []
    for i, ref in enumerate((own, right, left, far_a, far_b)):
        rows = ref.shape[0]
        at = (0, 512, 1024, 1536, 1536 + HALF)[i]
        copy = pltpu.make_async_copy(ref, cot.at[at : at + rows, :], sems.at[1 + i])
        copy.start()
        loads.append(copy)
    load_w.wait()
    shifts = (0, NEAR - 1, 1, 2)
    total = jnp.zeros((ROWS, FEAT), jnp.float32)
    for group, shift in enumerate(shifts):
        if group < 3:
            loads[group].wait()
        for far in range(FAR):
            if group == 3 and far in (0, 2):
                loads[3 + far // 2].wait()
            owner = far * NEAR + lax.rem(near + shift, NEAR)
            at = (group * FAR + far) * COLS
            rows = weights[pl.ds(pl.multiple_of(owner * COLS, COLS), COLS), :]
            total = total + lax.dot_general(
                cot[at : at + COLS, :], rows, (((0,), (0,)), ((), ())), preferred_element_type=jnp.float32
            )
    grad[...] = total
    out = pltpu.make_async_copy(grad, dnormed, sems.at[6])
    out.start()
    part = x[...].astype(jnp.float32) * gain[...].astype(jnp.float32) * total
    lanes = part[:, :COLS]
    for i in range(1, FEAT // COLS):
        lanes = lanes + part[:, COLS * i : COLS * (i + 1)]
    products[...] = jnp.sum(lanes.T, axis=0, keepdims=True)
    first = core == 0
    for group, shift in enumerate(shifts):
        for far in range(FAR):
            owner = far * NEAR + lax.rem(near + shift, NEAR)
            at = (group * FAR + far) * COLS
            term = jnp.dot(cot[at : at + COLS, :], normed[...], preferred_element_type=jnp.float32)
            to = pl.multiple_of(owner * (COLS // 2), COLS // 2)
            for half in range(2):
                low = term[64 * half : 64 * half + 32]
                high = term[64 * half + 32 : 64 * half + 64]
                keep[pl.ds(to + 32 * half, 32), :] = jnp.where(first, low, high)
                send[pl.ds(to + 32 * half, 32), :] = jnp.where(first, high, low).astype(jnp.bfloat16)
    out.wait()


def core_step(position, own, right, left, far_a, far_b, w_kv, x, gain, normed):
    any_space = pl.BlockSpec(memory_space=pltpu.HBM)
    vmem = pl.BlockSpec(memory_space=pltpu.VMEM)
    return pl.pallas_call(
        core_kernel,
        in_specs=[pl.BlockSpec(memory_space=pltpu.SMEM)] + [any_space] * 6 + [vmem] * 3,
        out_specs=[vmem, vmem, any_space, vmem],
        out_shape=[
            jax.ShapeDtypeStruct((KV // 2, FEAT), jnp.float32),
            jax.ShapeDtypeStruct((KV // 2, FEAT), jnp.bfloat16),
            jax.ShapeDtypeStruct((ROWS, FEAT), jnp.float32),
            jax.ShapeDtypeStruct((1, ROWS), jnp.float32),
        ],
        scratch_shapes=[
            pltpu.VMEM((KV, ROWS), jnp.bfloat16),
            pltpu.VMEM((KV, FEAT), jnp.bfloat16),
            pltpu.VMEM((ROWS, FEAT), jnp.float32),
            pltpu.SemaphoreType.DMA((7,)),
        ],
        compiler_params=pltpu.CompilerParams(vmem_limit_bytes=66500000),
        name="core_step",
    )(position, own, right, left, far_a, far_b, w_kv, x, gain, normed)


def sum_over(vector, axis, size):
    total = vector
    for shift in range(1, size):
        total = total + lax.ppermute(vector, axis, [(i, (i + shift) % size) for i in range(size)])
    return total


def tensor_sum(vector):
    return sum_over(sum_over(vector, "zh", FAR), "zl", NEAR)


def shards(layer_input, gain, w_kv, d_kv, destination):
    near = lax.axis_index("zl")
    core = lax.axis_index("core")

    spread = jnp.broadcast_to(d_kv.reshape(1, DP, 8, COLS), (FAR, DP, 8, COLS)).reshape(FAR * DP, 8, COLS)
    received = lax.all_to_all(spread, ("zh", "chip", "core"), split_axis=0, concat_axis=0, tiled=True)

    ids = jnp.arange(ROWS, dtype=jnp.int32)
    same = (destination[:, None] == destination[None, :]) & (ids[:, None] < ids[None, :])
    slot_rank = jnp.sum(same.astype(jnp.int32), axis=0)
    position = jnp.where(destination >= 0, destination * 8 + slot_rank, -1)
    onehot = (ids[:, None] == position[None, :]).astype(jnp.bfloat16)

    values = layer_input.astype(jnp.float32)
    gain_wide = gain.astype(jnp.float32)
    inverse = lax.rsqrt(tensor_sum(jnp.sum(values * values, axis=1)) / D + EPS)
    normed = (values * inverse[:, None] * gain_wide).astype(jnp.bfloat16)

    onehot, normed, inverse = lax.optimization_barrier((onehot, normed, inverse))

    right = [(i, (i + 1) % TP) for i in range(TP)]
    left = [(i, (i - 1) % TP) for i in range(TP)]
    own = place(received.reshape(FAR * ROWS, COLS), onehot)
    behind = lax.ppermute(own, Z, right)
    ahead = lax.ppermute(own, Z, left)
    far_a = lax.ppermute(behind[:HALF], Z, right)
    far_b = lax.ppermute(ahead[HALF:], Z, left)

    where = jnp.stack([near, core]).astype(jnp.int32)
    keep, send, dnormed, products = core_step(
        where, own, behind, ahead, far_a, far_b, w_kv, layer_input, gain[None, :], normed
    )

    taken = lax.ppermute(send, "core", [(0, 1), (1, 0)])
    pair = (keep + taken.astype(jnp.float32)).astype(jnp.bfloat16)
    pair, products = lax.optimization_barrier((pair, products))
    parts = lax.all_to_all(pair, "chip", split_axis=0, concat_axis=0, tiled=True)
    grad_weight = jnp.sum(parts.reshape(CHIPS, 32, FEAT).astype(jnp.float32), axis=0)

    mean_dot = tensor_sum(products[0]) / D
    grad_x = (inverse[:, None] * gain_wide * dnormed - values * (inverse**3 * mean_dot)[:, None]).astype(jnp.bfloat16)
    return (grad_x, grad_weight)


def solution(mesh):
    fine = Mesh(mesh.devices.reshape(CHIPS, 2, FAR, NEAR), ("chip", "core", "zh", "zl"))
    dp = ("chip", "core")
    return jax.shard_map(
        shards,
        mesh=fine,
        in_specs=(P(dp, Z), P(Z), P(None, Z), P(dp, Z), P(dp)),
        out_specs=(P(dp, Z), P(dp, Z)),
        check_vma=False,
    )
```

```python
import jax
import jax.numpy as jnp
from jax import lax
from jax.experimental import pallas as pl
from jax.experimental.pallas import tpu as pltpu
from jax.sharding import Mesh, PartitionSpec as P


D = 8192
EPS = 1e-06
ROWS = 512
FEAT = 512
COLS = 128
FAR = 4
NEAR = 4
TP = FAR * NEAR
CHIPS = 32
DP = 2 * CHIPS
HALF = FAR * COLS // 2
Z = ("zh", "zl")
TRANSPOSED = (((0,), (0,)), ((), ()))


def call(body, grid, inputs, outputs, shapes, flops, moved):
    return pl.pallas_call(
        body,
        grid_spec=pltpu.PrefetchScalarGridSpec(
            num_scalar_prefetch=1, grid=(grid,), in_specs=inputs, out_specs=outputs
        ),
        out_shape=shapes,
        cost_estimate=pl.CostEstimate(flops=flops, bytes_accessed=moved, transcendentals=0),
    )


def block(shape, index):
    return pl.BlockSpec(shape, index)


def fixed(shape):
    return pl.BlockSpec(shape, lambda i, where: (0,) * len(shape))


def rows_at(shape):
    return pl.BlockSpec(shape, lambda i, where: (i,) + (0,) * (len(shape) - 1))


def w_rows(shift, first=0):
    return pl.BlockSpec((COLS, FEAT), lambda i, where: ((first + i) * NEAR + lax.rem(where[0] + shift, NEAR), 0))


def place_kernel(where, received, onehot, out):
    picked = lax.dot_general(received[...], onehot[...], TRANSPOSED, preferred_element_type=jnp.float32)
    out[...] = picked.astype(jnp.bfloat16)


def place(where, received, onehot):
    return call(
        place_kernel,
        FAR,
        [rows_at((ROWS, COLS)), fixed((ROWS, ROWS))],
        rows_at((COLS, ROWS)),
        jax.ShapeDtypeStruct((FAR * COLS, ROWS), jnp.bfloat16),
        2 * FAR * ROWS * ROWS * COLS,
        3 * ROWS * ROWS * 2,
    )(where, received, onehot)


def grad_own_kernel(where, own, w, out):
    @pl.when(pl.program_id(0) == 0)
    def _():
        out[...] = jnp.zeros_like(out)

    out[...] += lax.dot_general(own[...], w[...], TRANSPOSED, preferred_element_type=jnp.float32)


def grad_own(where, own, w_kv):
    return call(
        grad_own_kernel,
        FAR,
        [rows_at((COLS, ROWS)), w_rows(0)],
        fixed((ROWS, FEAT)),
        jax.ShapeDtypeStruct((ROWS, FEAT), jnp.float32),
        2 * FAR * ROWS * FEAT * COLS,
        4 * ROWS * ROWS * 2,
    )(where, own, w_kv)


def grad_near_kernel(where, behind, ahead, w_behind, w_ahead, before, out):
    @pl.when(pl.program_id(0) == 0)
    def _():
        out[...] = before[...]

    term = lax.dot_general(behind[...], w_behind[...], TRANSPOSED, preferred_element_type=jnp.float32)
    term = term + lax.dot_general(ahead[...], w_ahead[...], TRANSPOSED, preferred_element_type=jnp.float32)
    out[...] += term


def grad_near(where, behind, ahead, w_kv, before):
    return call(
        grad_near_kernel,
        FAR,
        [rows_at((COLS, ROWS)), rows_at((COLS, ROWS)), w_rows(NEAR - 1), w_rows(1), fixed((ROWS, FEAT))],
        fixed((ROWS, FEAT)),
        jax.ShapeDtypeStruct((ROWS, FEAT), jnp.float32),
        4 * FAR * ROWS * FEAT * COLS,
        8 * ROWS * ROWS * 2,
    )(where, behind, ahead, w_kv, w_kv, before)


def grad_last_kernel(where, far_a, far_b, w_a, w_b, before, x, gain, out, products):
    @pl.when(pl.program_id(0) == 0)
    def _():
        out[...] = before[...]

    term = lax.dot_general(far_a[...], w_a[...], TRANSPOSED, preferred_element_type=jnp.float32)
    term = term + lax.dot_general(far_b[...], w_b[...], TRANSPOSED, preferred_element_type=jnp.float32)
    out[...] += term

    @pl.when(pl.program_id(0) == 1)
    def _():
        part = x[...].astype(jnp.float32) * gain[...].astype(jnp.float32) * out[...]
        lanes = part[:, :COLS]
        for i in range(1, FEAT // COLS):
            lanes = lanes + part[:, COLS * i : COLS * (i + 1)]
        products[...] = jnp.sum(lanes.T, axis=0, keepdims=True)


def grad_last(where, far_a, far_b, w_kv, before, x, gain):
    return call(
        grad_last_kernel,
        2,
        [
            rows_at((COLS, ROWS)),
            rows_at((COLS, ROWS)),
            w_rows(2),
            w_rows(2, 2),
            fixed((ROWS, FEAT)),
            fixed((ROWS, FEAT)),
            fixed((1, FEAT)),
        ],
        [fixed((ROWS, FEAT)), fixed((1, ROWS))],
        [jax.ShapeDtypeStruct((ROWS, FEAT), jnp.float32), jax.ShapeDtypeStruct((1, ROWS), jnp.float32)],
        2 * FAR * ROWS * FEAT * COLS,
        8 * ROWS * ROWS * 2,
    )(where, far_a, far_b, w_kv, w_kv, before, x, gain)


def split_rows(where, term):
    first = where[1] == 0
    low = jnp.concatenate([term[0:32], term[64:96]], axis=0)
    high = jnp.concatenate([term[32:64], term[96:128]], axis=0)
    return jnp.where(first, low, high), jnp.where(first, high, low).astype(jnp.bfloat16)


def weight_near_kernel(where, own, behind, ahead, normed, keep, send):
    for group, ref in enumerate((own, behind, ahead)):
        term = jnp.dot(ref[...], normed[...], preferred_element_type=jnp.float32)
        kept, sent = split_rows(where, term)
        keep[0, group] = kept
        send[0, group] = sent


def weight_near(where, own, behind, ahead, normed):
    spec = rows_at((1, 3, COLS // 2, FEAT))
    return call(
        weight_near_kernel,
        FAR,
        [rows_at((COLS, ROWS))] * 3 + [fixed((ROWS, FEAT))],
        [spec, spec],
        [
            jax.ShapeDtypeStruct((FAR, 3, COLS // 2, FEAT), jnp.float32),
            jax.ShapeDtypeStruct((FAR, 3, COLS // 2, FEAT), jnp.bfloat16),
        ],
        6 * FAR * ROWS * FEAT * COLS,
        12 * ROWS * ROWS * 2,
    )(where, own, behind, ahead, normed)


def weight_far_kernel(where, far_a, far_b, normed, keep, send):
    for group, ref in enumerate((far_a, far_b)):
        term = jnp.dot(ref[...], normed[...], preferred_element_type=jnp.float32)
        kept, sent = split_rows(where, term)
        keep[group, 0] = kept
        send[group, 0] = sent


def weight_far(where, far_a, far_b, normed):
    spec = block((2, 1, COLS // 2, FEAT), lambda i, where: (0, i, 0, 0))
    return call(
        weight_far_kernel,
        2,
        [rows_at((COLS, ROWS))] * 2 + [fixed((ROWS, FEAT))],
        [spec, spec],
        [
            jax.ShapeDtypeStruct((2, 2, COLS // 2, FEAT), jnp.float32),
            jax.ShapeDtypeStruct((2, 2, COLS // 2, FEAT), jnp.bfloat16),
        ],
        2 * FAR * ROWS * FEAT * COLS,
        5 * ROWS * ROWS * 2,
    )(where, far_a, far_b, normed)


def combine_kernel(where, keep_near, taken_near, keep_far, taken_far, out):
    for group, shift in enumerate((0, NEAR - 1, 1)):
        total = keep_near[0, group] + taken_near[0, group].astype(jnp.float32)
        out[0, lax.rem(where[0] + shift, NEAR)] = total.astype(jnp.bfloat16)
    total = keep_far[0] + taken_far[0].astype(jnp.float32)
    out[0, lax.rem(where[0] + 2, NEAR)] = total.astype(jnp.bfloat16)


def combine(where, keep_near, taken_near, keep_far, taken_far):
    near = rows_at((1, 3, COLS // 2, FEAT))
    far = rows_at((1, COLS // 2, FEAT))
    return call(
        combine_kernel,
        FAR,
        [near, near, far, far],
        rows_at((1, NEAR, COLS // 2, FEAT)),
        jax.ShapeDtypeStruct((FAR, NEAR, COLS // 2, FEAT), jnp.bfloat16),
        TP * COLS * FEAT,
        8 * ROWS * ROWS * 2,
    )(where, keep_near, taken_near, keep_far, taken_far)


def tensor_sum(vector):
    spread = jnp.broadcast_to(vector.reshape(1, ROWS), (TP, ROWS))
    return jnp.sum(lax.all_to_all(spread, Z, split_axis=0, concat_axis=0, tiled=True), axis=0)


def hop(array, step):
    return lax.ppermute(array, Z, [(i, (i + step) % TP) for i in range(TP)])


def swap(array):
    return lax.ppermute(array, "core", [(0, 1), (1, 0)])


def step(layer_input, gain, w_kv, d_kv, destination):
    where = jnp.stack([lax.axis_index("zl"), lax.axis_index("core")]).astype(jnp.int32)

    spread = jnp.broadcast_to(d_kv.reshape(1, DP, 8, COLS), (FAR, DP, 8, COLS)).reshape(FAR * DP, 8, COLS)
    received = lax.all_to_all(spread, ("zh", "chip", "core"), split_axis=0, concat_axis=0, tiled=True)

    ids = jnp.arange(ROWS, dtype=jnp.int32)
    same = (destination[:, None] == destination[None, :]) & (ids[:, None] < ids[None, :])
    slot_rank = jnp.sum(same.astype(jnp.int32), axis=0)
    position = jnp.where(destination >= 0, destination * 8 + slot_rank, -1)
    onehot = (ids[:, None] == position[None, :]).astype(jnp.bfloat16)

    values = layer_input.astype(jnp.float32)
    gain_wide = gain.astype(jnp.float32)
    squares = jnp.sum(values * values, axis=1)
    onehot, squares, where = lax.optimization_barrier((onehot, squares, where))

    own = place(where, received.reshape(FAR * ROWS, COLS), onehot)
    own, squares = lax.optimization_barrier((own, squares))
    behind = hop(own, 1)
    ahead = hop(own, -1)
    inverse = lax.rsqrt(tensor_sum(squares) / D + EPS)
    normed = (values * inverse[:, None] * gain_wide).astype(jnp.bfloat16)
    far_a = hop(behind[:HALF], 1)
    far_b = hop(ahead[HALF:], -1)

    grad = grad_own(where, own, w_kv)
    grad = grad_near(where, behind, ahead, w_kv, grad)
    keep_near, send_near = weight_near(where, own, behind, ahead, normed)
    taken_near = swap(send_near)
    dnormed, products = grad_last(where, far_a, far_b, w_kv, grad, layer_input, gain[None, :])
    mean_dot = tensor_sum(products) / D

    keep_far, send_far = weight_far(where, far_a, far_b, normed)
    taken_far = swap(send_far)
    shape = (FAR, COLS // 2, FEAT)
    pair = combine(where, keep_near, taken_near, keep_far.reshape(shape), taken_far.reshape(shape))
    pair, mean_dot, inverse, dnormed = lax.optimization_barrier((pair, mean_dot, inverse, dnormed))
    parts = lax.all_to_all(pair.reshape(CHIPS, 32, FEAT), "chip", split_axis=0, concat_axis=0, tiled=True)
    grad_weight = jnp.sum(parts.astype(jnp.float32), axis=0)
    grad_x = (inverse[:, None] * gain_wide * dnormed - values * (inverse**3 * mean_dot)[:, None]).astype(jnp.bfloat16)
    return (grad_x, grad_weight)


def solution(mesh):
    fine = Mesh(mesh.devices.reshape(CHIPS, 2, FAR, NEAR), ("chip", "core", "zh", "zl"))
    dp = ("chip", "core")
    return jax.shard_map(
        step,
        mesh=fine,
        in_specs=(P(dp, Z), P(Z), P(None, Z), P(dp, Z), P(dp)),
        out_specs=(P(dp, Z), P(dp, Z)),
        check_vma=False,
    )
```

```python
import jax
import jax.numpy as jnp
from jax import lax
from jax.experimental import pallas as pl
from jax.experimental.pallas import tpu as pltpu
from jax.sharding import Mesh, PartitionSpec as P


D = 8192
EPS = 1e-06
ROWS = 512
FEAT = 512
COLS = 128
FAR = 4
NEAR = 4
TP = FAR * NEAR
CHIPS = 32
HALF = FAR * COLS // 2
Z = ("zh", "zl")
TRANSPOSED = (((0,), (0,)), ((), ()))


def call(body, inputs, shapes, flops, moved, outputs=None, scratch=(), aliases=None):
    vmem = pl.BlockSpec(memory_space=pltpu.VMEM)
    specs = [pl.BlockSpec(memory_space=pltpu.SMEM)] + [vmem if s is None else s for s in inputs]
    return pl.pallas_call(
        body,
        in_specs=specs,
        out_specs=outputs if outputs is not None else jax.tree.map(lambda _: vmem, shapes),
        out_shape=shapes,
        scratch_shapes=scratch,
        input_output_aliases=aliases or {},
        cost_estimate=pl.CostEstimate(flops=flops, bytes_accessed=moved, transcendentals=0),
    )


def place_kernel(where, received, onehot, out):
    picked = lax.dot_general(received[...], onehot[...], TRANSPOSED, preferred_element_type=jnp.float32)
    out[...] = picked.astype(jnp.bfloat16)


def place(where, received, onehot):
    shape = jax.ShapeDtypeStruct((COLS, ROWS), jnp.bfloat16)
    return call(place_kernel, [None] * 2, shape, 2 * ROWS * ROWS * COLS, ROWS * ROWS * 3)(where, received, onehot)


def gradient(where, total, blocks, w):
    for ref, at, shift, far in blocks:
        owner = far * NEAR + lax.rem(where[0] + shift, NEAR)
        rows = w[pl.ds(pl.multiple_of(owner * COLS, COLS), COLS), :]
        term = lax.dot_general(ref[at : at + COLS, :], rows, TRANSPOSED, preferred_element_type=jnp.float32)
        total = term if total is None else total + term
    return total


def grad_own_kernel(where, own, w, out):
    out[...] = gradient(where, None, [(own, COLS * far, 0, far) for far in range(FAR)], w)


def grad_own(where, own, w_kv):
    shape = jax.ShapeDtypeStruct((ROWS, FEAT), jnp.float32)
    flops = 2 * FAR * ROWS * FEAT * COLS
    return call(grad_own_kernel, [None] * 2, shape, flops, 14 * ROWS * FEAT)(where, own, w_kv)


def grad_rest_kernel(where, behind, ahead, far_a, far_b, w, before, x, gain, out, products):
    blocks = [(behind, COLS * far, NEAR - 1, far) for far in range(FAR)]
    blocks += [(ahead, COLS * far, 1, far) for far in range(FAR)]
    blocks += [(far_a, COLS * far, 2, far) for far in range(2)]
    blocks += [(far_b, COLS * far, 2, 2 + far) for far in range(2)]
    total = gradient(where, before[...], blocks, w)
    out[...] = total
    part = x[...].astype(jnp.float32) * gain[...].astype(jnp.float32) * total
    lanes = part[:, :COLS]
    for i in range(1, FEAT // COLS):
        lanes = lanes + part[:, COLS * i : COLS * (i + 1)]
    products[...] = jnp.sum(lanes.T, axis=0, keepdims=True)


def grad_rest(where, behind, ahead, far_a, far_b, w_kv, before, x, gain):
    shapes = [jax.ShapeDtypeStruct((ROWS, FEAT), jnp.float32), jax.ShapeDtypeStruct((1, ROWS), jnp.float32)]
    flops = 6 * FAR * ROWS * FEAT * COLS
    return call(grad_rest_kernel, [None] * 8, shapes, flops, 24 * ROWS * FEAT)(
        where, behind, ahead, far_a, far_b, w_kv, before, x, gain
    )


def split_rows(where, term):
    first = where[1] == 0
    low = jnp.concatenate([term[0:32], term[64:96]], axis=0)
    high = jnp.concatenate([term[32:64], term[96:128]], axis=0)
    return jnp.where(first, low, high), jnp.where(first, high, low).astype(jnp.bfloat16)


def weight_near_kernel(where, own, behind, ahead, normed, keep, send):
    for group, ref in enumerate((own, behind, ahead)):
        for far in range(FAR):
            term = jnp.dot(ref[COLS * far : COLS * (far + 1), :], normed[...], preferred_element_type=jnp.float32)
            kept, sent = split_rows(where, term)
            keep[far, group] = kept
            send[far, group] = sent


def weight_near(where, own, behind, ahead, normed):
    shapes = [jax.ShapeDtypeStruct((FAR, 3, COLS // 2, FEAT), kind) for kind in (jnp.float32, jnp.bfloat16)]
    flops = 6 * FAR * ROWS * FEAT * COLS
    return call(weight_near_kernel, [None] * 4, shapes, flops, 18 * ROWS * FEAT)(where, own, behind, ahead, normed)


def weight_far_kernel(where, far_a, far_b, normed, keep, send):
    for far in range(FAR):
        ref, at = (far_a, far_b)[far // 2], COLS * (far % 2)
        term = jnp.dot(ref[at : at + COLS, :], normed[...], preferred_element_type=jnp.float32)
        kept, sent = split_rows(where, term)
        keep[far] = kept
        send[far] = sent


def weight_far(where, far_a, far_b, normed):
    shapes = [jax.ShapeDtypeStruct((FAR, COLS // 2, FEAT), kind) for kind in (jnp.float32, jnp.bfloat16)]
    flops = 2 * FAR * ROWS * FEAT * COLS
    return call(weight_far_kernel, [None] * 3, shapes, flops, 8 * ROWS * FEAT)(where, far_a, far_b, normed)


def combine_near_kernel(where, keep, taken, out, total, sems):
    copies = []
    for far in range(FAR):
        for group, shift in enumerate((0, NEAR - 1, 1)):
            total[far, group] = (keep[far, group] + taken[far, group].astype(jnp.float32)).astype(jnp.bfloat16)
            to = out.at[far, lax.rem(where[0] + shift, NEAR)]
            copies.append(pltpu.make_async_copy(total.at[far, group], to, sems.at[far, group]))
            copies[-1].start()
    for copy in copies:
        copy.wait()


def combine_near(where, keep, taken):
    return call(
        combine_near_kernel,
        [None] * 2,
        jax.ShapeDtypeStruct((FAR, NEAR, COLS // 2, FEAT), jnp.bfloat16),
        3 * FAR * COLS * FEAT,
        12 * ROWS * FEAT,
        outputs=pl.BlockSpec(memory_space=pltpu.HBM),
        scratch=[pltpu.VMEM((FAR, 3, COLS // 2, FEAT), jnp.bfloat16), pltpu.SemaphoreType.DMA((FAR, 3))],
    )(where, keep, taken)


def combine_far_kernel(where, keep, taken, placed, out, total, sems):
    copies = []
    for far in range(FAR):
        total[far] = (keep[far] + taken[far].astype(jnp.float32)).astype(jnp.bfloat16)
        to = out.at[far, lax.rem(where[0] + 2, NEAR)]
        copies.append(pltpu.make_async_copy(total.at[far], to, sems.at[far]))
        copies[-1].start()
    for copy in copies:
        copy.wait()


def combine_far(where, keep, taken, placed):
    hbm = pl.BlockSpec(memory_space=pltpu.HBM)
    return call(
        combine_far_kernel,
        [None, None, hbm],
        jax.ShapeDtypeStruct(placed.shape, placed.dtype),
        FAR * COLS * FEAT,
        5 * ROWS * FEAT,
        outputs=hbm,
        scratch=[pltpu.VMEM((FAR, COLS // 2, FEAT), jnp.bfloat16), pltpu.SemaphoreType.DMA((FAR,))],
        aliases={3: 0},
    )(where, keep, taken, placed)


def tensor_sum(vector):
    spread = jnp.broadcast_to(vector.reshape(1, ROWS), (TP, ROWS))
    return jnp.sum(lax.all_to_all(spread, Z, split_axis=0, concat_axis=0, tiled=True), axis=0)


def hop(array, step):
    return lax.ppermute(array, Z, [(i, (i + step) % TP) for i in range(TP)])


def swap(array):
    return lax.ppermute(array, "core", [(0, 1), (1, 0)])


def ladder(vector):
    for distance in (8, 4, 2, 1):
        vector = vector + hop(vector, distance)
    return vector


def step(layer_input, gain, w_kv, d_kv, destination):
    where = jnp.stack([lax.axis_index("zl"), lax.axis_index("core")]).astype(jnp.int32)
    received = lax.all_to_all(d_kv, ("chip", "core"), split_axis=0, concat_axis=0, tiled=True)

    ids = jnp.arange(ROWS, dtype=jnp.int32)
    same = (destination[:, None] == destination[None, :]) & (ids[:, None] < ids[None, :])
    slot_rank = jnp.sum(same.astype(jnp.int32), axis=0)
    position = jnp.where(destination >= 0, destination * 8 + slot_rank, -1)
    onehot = (ids[:, None] == position[None, :]).astype(jnp.bfloat16)

    values = layer_input.astype(jnp.float32)
    gain_wide = gain.astype(jnp.float32)
    squares = jnp.sum(values * values, axis=1)
    onehot, squares, where = lax.optimization_barrier((onehot, squares, where))

    block = place(where, received, onehot)
    copies = jnp.broadcast_to(block[None], (FAR, COLS, ROWS))
    own = lax.all_to_all(copies, "zh", split_axis=0, concat_axis=0, tiled=True).reshape(FAR * COLS, ROWS)
    own, squares = lax.optimization_barrier((own, squares))
    behind = hop(own, 1)
    ahead = hop(own, -1)
    inverse = lax.rsqrt(tensor_sum(squares) / D + EPS)
    normed = (values * inverse[:, None] * gain_wide).astype(jnp.bfloat16)
    far_a = hop(behind[:HALF], 1)
    far_b = hop(ahead[HALF:], -1)

    grad = grad_own(where, own, w_kv)
    keep_near, send_near = weight_near(where, own, behind, ahead, normed)
    taken_near = swap(send_near)
    placed = combine_near(where, keep_near, taken_near)
    keep_far, send_far = weight_far(where, far_a, far_b, normed)
    taken_far = swap(send_far)
    pair = combine_far(where, keep_far, taken_far, placed)
    pair, x, inverse = lax.optimization_barrier((pair, layer_input, inverse))
    parts = lax.all_to_all(pair.reshape(CHIPS, 32, FEAT), "chip", split_axis=0, concat_axis=0, tiled=True)
    grad_weight = jnp.sum(parts.astype(jnp.float32), axis=0)

    dnormed, products = grad_rest(where, behind, ahead, far_a, far_b, w_kv, grad, x, gain[None, :])
    mean_dot = ladder(products[0]) / D
    along = x.astype(jnp.float32) * (inverse**3 * mean_dot)[:, None]
    grad_x = (inverse[:, None] * gain_wide * dnormed - along).astype(jnp.bfloat16)
    return (grad_x, grad_weight)


def solution(mesh):
    fine = Mesh(mesh.devices.reshape(CHIPS, 2, FAR, NEAR), ("chip", "core", "zh", "zl"))
    dp = ("chip", "core")
    return jax.shard_map(
        step,
        mesh=fine,
        in_specs=(P(dp, Z), P(Z), P(None, Z), P(dp, Z), P(dp)),
        out_specs=(P(dp, Z), P(dp, Z)),
        check_vma=False,
    )
```

```python
import jax
import jax.numpy as jnp
from jax import lax
from jax.experimental import pallas as pl
from jax.experimental.pallas import tpu as pltpu
from jax.sharding import Mesh, PartitionSpec as P


D = 8192
EPS = 1e-06
ROWS = 512
FEAT = 512
COLS = 128
FAR = 4
NEAR = 4
TP = FAR * NEAR
CHIPS = 32
HALF = FAR * COLS // 2
GRANT = 24 * 1024 * 1024
Z = ("zh", "zl")
TRANSPOSED = (((0,), (0,)), ((), ()))


def call(body, inputs, shapes, flops, moved, outputs=None, scratch=(), aliases=None):
    vmem = pl.BlockSpec(memory_space=pltpu.VMEM)
    specs = [pl.BlockSpec(memory_space=pltpu.SMEM)] + [vmem if s is None else s for s in inputs]
    return pl.pallas_call(
        body,
        in_specs=specs,
        out_specs=outputs if outputs is not None else jax.tree.map(lambda _: vmem, shapes),
        out_shape=shapes,
        scratch_shapes=scratch,
        input_output_aliases=aliases or {},
        cost_estimate=pl.CostEstimate(flops=flops, bytes_accessed=moved, transcendentals=0),
        compiler_params=pltpu.CompilerParams(vmem_limit_bytes=GRANT),
    )


def place_kernel(where, received, onehot, out):
    picked = lax.dot_general(received[...], onehot[...], TRANSPOSED, preferred_element_type=jnp.float32)
    out[...] = picked.astype(jnp.bfloat16)


def place(where, received, onehot):
    shape = jax.ShapeDtypeStruct((COLS, ROWS), jnp.bfloat16)
    return call(place_kernel, [None] * 2, shape, 2 * ROWS * ROWS * COLS, ROWS * ROWS * 3)(where, received, onehot)


def gradient(where, total, blocks, w):
    for ref, at, shift, far in blocks:
        owner = far * NEAR + lax.rem(where[0] + shift, NEAR)
        rows = w[pl.ds(pl.multiple_of(owner * COLS, COLS), COLS), :]
        term = lax.dot_general(ref[at : at + COLS, :], rows, TRANSPOSED, preferred_element_type=jnp.float32)
        total = term if total is None else total + term
    return total


def grad_own_kernel(where, own, w, out):
    out[...] = gradient(where, None, [(own, COLS * far, 0, far) for far in range(FAR)], w)


def grad_own(where, own, w_kv):
    shape = jax.ShapeDtypeStruct((ROWS, FEAT), jnp.float32)
    flops = 2 * FAR * ROWS * FEAT * COLS
    return call(grad_own_kernel, [None] * 2, shape, flops, 14 * ROWS * FEAT)(where, own, w_kv)


def grad_rest_kernel(where, behind, ahead, far_a, far_b, w, before, x, gain, out, products):
    blocks = [(behind, COLS * far, NEAR - 1, far) for far in range(FAR)]
    blocks += [(ahead, COLS * far, 1, far) for far in range(FAR)]
    blocks += [(far_a, COLS * far, 2, far) for far in range(2)]
    blocks += [(far_b, COLS * far, 2, 2 + far) for far in range(2)]
    total = gradient(where, before[...], blocks, w)
    out[...] = total
    part = x[...].astype(jnp.float32) * gain[...].astype(jnp.float32) * total
    lanes = part[:, :COLS]
    for i in range(1, FEAT // COLS):
        lanes = lanes + part[:, COLS * i : COLS * (i + 1)]
    products[...] = jnp.sum(lanes.T, axis=0, keepdims=True)


def grad_rest(where, behind, ahead, far_a, far_b, w_kv, before, x, gain):
    shapes = [jax.ShapeDtypeStruct((ROWS, FEAT), jnp.float32), jax.ShapeDtypeStruct((1, ROWS), jnp.float32)]
    flops = 6 * FAR * ROWS * FEAT * COLS
    return call(grad_rest_kernel, [None] * 8, shapes, flops, 24 * ROWS * FEAT)(
        where, behind, ahead, far_a, far_b, w_kv, before, x, gain
    )


def split_rows(where, term):
    first = where[1] == 0
    low = jnp.concatenate([term[0:32], term[64:96]], axis=0)
    high = jnp.concatenate([term[32:64], term[96:128]], axis=0)
    return jnp.where(first, low, high), jnp.where(first, high, low).astype(jnp.bfloat16)


def weight_near_kernel(where, own, behind, ahead, normed, keep, send):
    for group, ref in enumerate((own, behind, ahead)):
        for far in range(FAR):
            term = jnp.dot(ref[COLS * far : COLS * (far + 1), :], normed[...], preferred_element_type=jnp.float32)
            kept, sent = split_rows(where, term)
            keep[far, group] = kept
            send[far, group] = sent


def weight_near(where, own, behind, ahead, normed):
    shapes = [jax.ShapeDtypeStruct((FAR, 3, COLS // 2, FEAT), kind) for kind in (jnp.float32, jnp.bfloat16)]
    flops = 6 * FAR * ROWS * FEAT * COLS
    return call(weight_near_kernel, [None] * 4, shapes, flops, 18 * ROWS * FEAT)(where, own, behind, ahead, normed)


def weight_far_kernel(where, far_a, far_b, normed, keep, send):
    for far in range(FAR):
        ref, at = (far_a, far_b)[far // 2], COLS * (far % 2)
        term = jnp.dot(ref[at : at + COLS, :], normed[...], preferred_element_type=jnp.float32)
        kept, sent = split_rows(where, term)
        keep[far] = kept
        send[far] = sent


def weight_far(where, far_a, far_b, normed):
    shapes = [jax.ShapeDtypeStruct((FAR, COLS // 2, FEAT), kind) for kind in (jnp.float32, jnp.bfloat16)]
    flops = 2 * FAR * ROWS * FEAT * COLS
    return call(weight_far_kernel, [None] * 3, shapes, flops, 8 * ROWS * FEAT)(where, far_a, far_b, normed)


def combine_near_kernel(where, keep, taken, out, total, sems):
    copies = []
    for far in range(FAR):
        for group, shift in enumerate((0, NEAR - 1, 1)):
            total[far, group] = (keep[far, group] + taken[far, group].astype(jnp.float32)).astype(jnp.bfloat16)
            to = out.at[far, lax.rem(where[0] + shift, NEAR)]
            copies.append(pltpu.make_async_copy(total.at[far, group], to, sems.at[far, group]))
            copies[-1].start()
    for copy in copies:
        copy.wait()


def combine_near(where, keep, taken):
    return call(
        combine_near_kernel,
        [None] * 2,
        jax.ShapeDtypeStruct((FAR, NEAR, COLS // 2, FEAT), jnp.bfloat16),
        3 * FAR * COLS * FEAT,
        12 * ROWS * FEAT,
        outputs=pl.BlockSpec(memory_space=pltpu.HBM),
        scratch=[pltpu.VMEM((FAR, 3, COLS // 2, FEAT), jnp.bfloat16), pltpu.SemaphoreType.DMA((FAR, 3))],
    )(where, keep, taken)


def combine_far_kernel(where, keep, taken, placed, out, total, sems):
    copies = []
    for far in range(FAR):
        total[far] = (keep[far] + taken[far].astype(jnp.float32)).astype(jnp.bfloat16)
        to = out.at[far, lax.rem(where[0] + 2, NEAR)]
        copies.append(pltpu.make_async_copy(total.at[far], to, sems.at[far]))
        copies[-1].start()
    for copy in copies:
        copy.wait()


def combine_far(where, keep, taken, placed):
    hbm = pl.BlockSpec(memory_space=pltpu.HBM)
    return call(
        combine_far_kernel,
        [None, None, hbm],
        jax.ShapeDtypeStruct(placed.shape, placed.dtype),
        FAR * COLS * FEAT,
        5 * ROWS * FEAT,
        outputs=hbm,
        scratch=[pltpu.VMEM((FAR, COLS // 2, FEAT), jnp.bfloat16), pltpu.SemaphoreType.DMA((FAR,))],
        aliases={3: 0},
    )(where, keep, taken, placed)


def tensor_sum(vector):
    spread = jnp.broadcast_to(vector.reshape(1, ROWS), (TP, ROWS))
    return jnp.sum(lax.all_to_all(spread, Z, split_axis=0, concat_axis=0, tiled=True), axis=0)


def hop(array, step):
    return lax.ppermute(array, Z, [(i, (i + step) % TP) for i in range(TP)])


def swap(array):
    return lax.ppermute(array, "core", [(0, 1), (1, 0)])


def gather_sum(vector):
    return jnp.sum(lax.all_gather(vector, Z, axis=0, tiled=True), axis=0)


def step(layer_input, gain, w_kv, d_kv, destination):
    where = jnp.stack([lax.axis_index("zl"), lax.axis_index("core")]).astype(jnp.int32)
    received = lax.all_to_all(d_kv, ("chip", "core"), split_axis=0, concat_axis=0, tiled=True)

    ids = jnp.arange(ROWS, dtype=jnp.int32)
    same = (destination[:, None] == destination[None, :]) & (ids[:, None] < ids[None, :])
    slot_rank = jnp.sum(same.astype(jnp.int32), axis=0)
    position = jnp.where(destination >= 0, destination * 8 + slot_rank, -1)
    onehot = (ids[:, None] == position[None, :]).astype(jnp.bfloat16)

    values = layer_input.astype(jnp.float32)
    gain_wide = gain.astype(jnp.float32)
    squares = jnp.sum(values * values, axis=1)
    onehot, squares, where = lax.optimization_barrier((onehot, squares, where))

    block = place(where, received, onehot)
    own = lax.all_gather(block, "zh", axis=0, tiled=True)
    own, squares = lax.optimization_barrier((own, squares))
    behind = hop(own, 1)
    ahead = hop(own, -1)
    inverse = lax.rsqrt(tensor_sum(squares) / D + EPS)
    normed = (values * inverse[:, None] * gain_wide).astype(jnp.bfloat16)
    far_a = hop(behind[:HALF], 1)
    far_b = hop(ahead[HALF:], -1)

    grad = grad_own(where, own, w_kv)
    keep_near, send_near = weight_near(where, own, behind, ahead, normed)
    taken_near = swap(send_near)
    placed = combine_near(where, keep_near, taken_near)
    keep_far, send_far = weight_far(where, far_a, far_b, normed)
    taken_far = swap(send_far)
    pair = combine_far(where, keep_far, taken_far, placed)
    pair, x, inverse = lax.optimization_barrier((pair, layer_input, inverse))
    parts = lax.all_to_all(pair.reshape(CHIPS, 32, FEAT), "chip", split_axis=0, concat_axis=0, tiled=True)
    grad_weight = jnp.sum(parts.astype(jnp.float32), axis=0)

    dnormed, products = grad_rest(where, behind, ahead, far_a, far_b, w_kv, grad, x, gain[None, :])
    mean_dot = gather_sum(products) / D
    along = x.astype(jnp.float32) * (inverse**3 * mean_dot)[:, None]
    grad_x = (inverse[:, None] * gain_wide * dnormed - along).astype(jnp.bfloat16)
    return (grad_x, grad_weight)


def solution(mesh):
    fine = Mesh(mesh.devices.reshape(CHIPS, 2, FAR, NEAR), ("chip", "core", "zh", "zl"))
    dp = ("chip", "core")
    return jax.shard_map(
        step,
        mesh=fine,
        in_specs=(P(dp, Z), P(Z), P(None, Z), P(dp, Z), P(dp)),
        out_specs=(P(dp, Z), P(dp, Z)),
        check_vma=False,
    )
```

```python
import jax
import jax.numpy as jnp
from jax import lax
from jax.experimental import pallas as pl
from jax.experimental.pallas import tpu as pltpu
from jax.sharding import Mesh, PartitionSpec as P


D = 8192
EPS = 1e-06
ROWS = 512
FEAT = 512
COLS = 128
FAR = 4
NEAR = 4
TP = FAR * NEAR
CHIPS = 32
HALF = FAR * COLS // 2
GRANT = 24 * 1024 * 1024
Z = ("zh", "zl")
TRANSPOSED = (((0,), (0,)), ((), ()))


def call(body, inputs, shapes, flops, moved, outputs=None, scratch=(), aliases=None):
    vmem = pl.BlockSpec(memory_space=pltpu.VMEM)
    specs = [pl.BlockSpec(memory_space=pltpu.SMEM)] + [vmem if s is None else s for s in inputs]
    return pl.pallas_call(
        body,
        in_specs=specs,
        out_specs=outputs if outputs is not None else jax.tree.map(lambda _: vmem, shapes),
        out_shape=shapes,
        scratch_shapes=scratch,
        input_output_aliases=aliases or {},
        cost_estimate=pl.CostEstimate(flops=flops, bytes_accessed=moved, transcendentals=0),
        compiler_params=pltpu.CompilerParams(vmem_limit_bytes=GRANT),
    )


def place_kernel(where, received, onehot, out):
    picked = lax.dot_general(received[...], onehot[...], TRANSPOSED, preferred_element_type=jnp.float32)
    out[...] = picked.astype(jnp.bfloat16)


def place(where, received, onehot):
    shape = jax.ShapeDtypeStruct((COLS, ROWS), jnp.bfloat16)
    return call(place_kernel, [None] * 2, shape, 2 * ROWS * ROWS * COLS, ROWS * ROWS * 3)(where, received, onehot)


def fetch(where, w, pieces, rows, sems):
    copies = []
    for i, (_, _, shift, far) in enumerate(pieces):
        owner = far * NEAR + lax.rem(where[0] + shift, NEAR)
        source = w.at[pl.ds(pl.multiple_of(owner * COLS, COLS), COLS), :]
        copies.append(pltpu.make_async_copy(source, rows.at[i], sems.at[i]))
        copies[-1].start()
    return copies


def gradient(where, w, pieces, rows, sems, total):
    copies = fetch(where, w, pieces, rows, sems)
    for i, (ref, at, _, _) in enumerate(pieces):
        copies[i].wait()
        term = lax.dot_general(ref[at : at + COLS, :], rows[i], TRANSPOSED, preferred_element_type=jnp.float32)
        total = term if total is None else total + term
    return total


def grad_near_kernel(where, own, behind, ahead, w, out, rows, sems):
    pieces = [
        (ref, COLS * far, shift, far)
        for ref, shift in ((own, 0), (behind, NEAR - 1), (ahead, 1))
        for far in range(FAR)
    ]
    out[...] = gradient(where, w, pieces, rows, sems, None)


def w_scratch(count):
    return [pltpu.VMEM((count, COLS, FEAT), jnp.bfloat16), pltpu.SemaphoreType.DMA((count,))]


def grad_near(where, own, behind, ahead, w_kv):
    shape = jax.ShapeDtypeStruct((ROWS, FEAT), jnp.float32)
    flops = 6 * FAR * ROWS * FEAT * COLS
    hbm = pl.BlockSpec(memory_space=pltpu.HBM)
    return call(
        grad_near_kernel, [None] * 3 + [hbm], shape, flops, 14 * ROWS * FEAT, scratch=w_scratch(3 * FAR)
    )(where, own, behind, ahead, w_kv)


def grad_far_kernel(where, far_a, far_b, w, before, x, gain, out, products, rows, sems):
    pieces = [(ref, COLS * (far % 2), 2, far) for far, ref in enumerate((far_a, far_a, far_b, far_b))]
    total = gradient(where, w, pieces, rows, sems, before[...])
    out[...] = total
    part = x[...].astype(jnp.float32) * gain[...].astype(jnp.float32) * total
    lanes = part[:, :COLS]
    for i in range(1, FEAT // COLS):
        lanes = lanes + part[:, COLS * i : COLS * (i + 1)]
    products[...] = jnp.sum(lanes.T, axis=0, keepdims=True)


def grad_far(where, far_a, far_b, w_kv, before, x, gain):
    shapes = [jax.ShapeDtypeStruct((ROWS, FEAT), jnp.float32), jax.ShapeDtypeStruct((1, ROWS), jnp.float32)]
    flops = 2 * FAR * ROWS * FEAT * COLS
    hbm = pl.BlockSpec(memory_space=pltpu.HBM)
    return call(
        grad_far_kernel, [None, None, hbm, None, None, None], shapes, flops, 14 * ROWS * FEAT, scratch=w_scratch(FAR)
    )(where, far_a, far_b, w_kv, before, x, gain)


def split_rows(where, term):
    first = where[1] == 0
    low = jnp.concatenate([term[0:32], term[64:96]], axis=0)
    high = jnp.concatenate([term[32:64], term[96:128]], axis=0)
    return jnp.where(first, low, high), jnp.where(first, high, low).astype(jnp.bfloat16)


def weight_near_kernel(where, own, behind, ahead, normed, keep, send):
    for group, ref in enumerate((own, behind, ahead)):
        for far in range(FAR):
            term = jnp.dot(ref[COLS * far : COLS * (far + 1), :], normed[...], preferred_element_type=jnp.float32)
            kept, sent = split_rows(where, term)
            keep[far, group] = kept
            send[far, group] = sent


def weight_near(where, own, behind, ahead, normed):
    shapes = [jax.ShapeDtypeStruct((FAR, 3, COLS // 2, FEAT), kind) for kind in (jnp.float32, jnp.bfloat16)]
    flops = 6 * FAR * ROWS * FEAT * COLS
    return call(weight_near_kernel, [None] * 4, shapes, flops, 18 * ROWS * FEAT)(where, own, behind, ahead, normed)


def weight_far_kernel(where, far_a, far_b, normed, keep, send):
    for far in range(FAR):
        ref, at = (far_a, far_b)[far // 2], COLS * (far % 2)
        term = jnp.dot(ref[at : at + COLS, :], normed[...], preferred_element_type=jnp.float32)
        kept, sent = split_rows(where, term)
        keep[far] = kept
        send[far] = sent


def weight_far(where, far_a, far_b, normed):
    shapes = [jax.ShapeDtypeStruct((FAR, COLS // 2, FEAT), kind) for kind in (jnp.float32, jnp.bfloat16)]
    flops = 2 * FAR * ROWS * FEAT * COLS
    return call(weight_far_kernel, [None] * 3, shapes, flops, 8 * ROWS * FEAT)(where, far_a, far_b, normed)


def combine_near_kernel(where, keep, taken, out, total, sems):
    copies = []
    for far in range(FAR):
        for group, shift in enumerate((0, NEAR - 1, 1)):
            total[far, group] = (keep[far, group] + taken[far, group].astype(jnp.float32)).astype(jnp.bfloat16)
            to = out.at[far, lax.rem(where[0] + shift, NEAR)]
            copies.append(pltpu.make_async_copy(total.at[far, group], to, sems.at[far, group]))
            copies[-1].start()
    for copy in copies:
        copy.wait()


def combine_near(where, keep, taken):
    return call(
        combine_near_kernel,
        [None] * 2,
        jax.ShapeDtypeStruct((FAR, NEAR, COLS // 2, FEAT), jnp.bfloat16),
        3 * FAR * COLS * FEAT,
        12 * ROWS * FEAT,
        outputs=pl.BlockSpec(memory_space=pltpu.HBM),
        scratch=[pltpu.VMEM((FAR, 3, COLS // 2, FEAT), jnp.bfloat16), pltpu.SemaphoreType.DMA((FAR, 3))],
    )(where, keep, taken)


def combine_far_kernel(where, keep, taken, placed, out, total, sems):
    copies = []
    for far in range(FAR):
        total[far] = (keep[far] + taken[far].astype(jnp.float32)).astype(jnp.bfloat16)
        to = out.at[far, lax.rem(where[0] + 2, NEAR)]
        copies.append(pltpu.make_async_copy(total.at[far], to, sems.at[far]))
        copies[-1].start()
    for copy in copies:
        copy.wait()


def combine_far(where, keep, taken, placed):
    hbm = pl.BlockSpec(memory_space=pltpu.HBM)
    return call(
        combine_far_kernel,
        [None, None, hbm],
        jax.ShapeDtypeStruct(placed.shape, placed.dtype),
        FAR * COLS * FEAT,
        5 * ROWS * FEAT,
        outputs=hbm,
        scratch=[pltpu.VMEM((FAR, COLS // 2, FEAT), jnp.bfloat16), pltpu.SemaphoreType.DMA((FAR,))],
        aliases={3: 0},
    )(where, keep, taken, placed)


def tensor_sum(vector):
    spread = jnp.broadcast_to(vector.reshape(1, ROWS), (TP, ROWS))
    return jnp.sum(lax.all_to_all(spread, Z, split_axis=0, concat_axis=0, tiled=True), axis=0)


def hop(array, step):
    return lax.ppermute(array, Z, [(i, (i + step) % TP) for i in range(TP)])


def swap(array):
    return lax.ppermute(array, "core", [(0, 1), (1, 0)])


def gather_sum(vector):
    return jnp.sum(lax.all_gather(vector, Z, axis=0, tiled=True), axis=0)


def step(layer_input, gain, w_kv, d_kv, destination):
    w_kv = pltpu.with_memory_space_constraint(w_kv, pltpu.HBM)
    where = jnp.stack([lax.axis_index("zl"), lax.axis_index("core")]).astype(jnp.int32)
    received = lax.all_to_all(d_kv, ("chip", "core"), split_axis=0, concat_axis=0, tiled=True)

    ids = jnp.arange(ROWS, dtype=jnp.int32)
    same = (destination[:, None] == destination[None, :]) & (ids[:, None] < ids[None, :])
    slot_rank = jnp.sum(same.astype(jnp.int32), axis=0)
    position = jnp.where(destination >= 0, destination * 8 + slot_rank, -1)
    onehot = (ids[:, None] == position[None, :]).astype(jnp.bfloat16)

    values = layer_input.astype(jnp.float32)
    gain_wide = gain.astype(jnp.float32)
    squares = jnp.sum(values * values, axis=1)
    onehot, squares, where = lax.optimization_barrier((onehot, squares, where))

    block = place(where, received, onehot)
    own = lax.all_gather(block, "zh", axis=0, tiled=True)
    own, squares = lax.optimization_barrier((own, squares))
    behind = hop(own, 1)
    ahead = hop(own, -1)
    inverse = lax.rsqrt(tensor_sum(squares) / D + EPS)
    normed = (values * inverse[:, None] * gain_wide).astype(jnp.bfloat16)
    far_a = hop(behind[:HALF], 1)
    far_b = hop(ahead[HALF:], -1)

    grad = grad_near(where, own, behind, ahead, w_kv)
    keep_near, send_near = weight_near(where, own, behind, ahead, normed)
    taken_near = swap(send_near)
    placed = combine_near(where, keep_near, taken_near)
    keep_far, send_far = weight_far(where, far_a, far_b, normed)
    taken_far = swap(send_far)
    pair = combine_far(where, keep_far, taken_far, placed)
    pair, x, inverse = lax.optimization_barrier((pair, layer_input, inverse))
    parts = lax.all_to_all(pair.reshape(CHIPS, 32, FEAT), "chip", split_axis=0, concat_axis=0, tiled=True)
    grad_weight = jnp.sum(parts.astype(jnp.float32), axis=0)

    dnormed, products = grad_far(where, far_a, far_b, w_kv, grad, x, gain[None, :])
    mean_dot = gather_sum(products) / D
    along = x.astype(jnp.float32) * (inverse**3 * mean_dot)[:, None]
    grad_x = (inverse[:, None] * gain_wide * dnormed - along).astype(jnp.bfloat16)
    return (grad_x, grad_weight)


def solution(mesh):
    fine = Mesh(mesh.devices.reshape(CHIPS, 2, FAR, NEAR), ("chip", "core", "zh", "zl"))
    dp = ("chip", "core")
    return jax.shard_map(
        step,
        mesh=fine,
        in_specs=(P(dp, Z), P(Z), P(None, Z), P(dp, Z), P(dp)),
        out_specs=(P(dp, Z), P(dp, Z)),
        check_vma=False,
    )
```

```python
import jax
import jax.numpy as jnp
from jax import lax
from jax.experimental import pallas as pl
from jax.experimental.pallas import tpu as pltpu
from jax.sharding import Mesh, PartitionSpec as P


D = 8192
EPS = 1e-06
ROWS = 512
FEAT = 512
COLS = 128
FAR = 4
NEAR = 4
TP = FAR * NEAR
CHIPS = 32
HALF = FAR * COLS // 2
GRANT = 24 * 1024 * 1024
Z = ("zh", "zl")
TRANSPOSED = (((0,), (0,)), ((), ()))


def call(body, inputs, shapes, flops, moved, outputs=None, scratch=(), aliases=None):
    vmem = pl.BlockSpec(memory_space=pltpu.VMEM)
    specs = [pl.BlockSpec(memory_space=pltpu.SMEM)] + [vmem if s is None else s for s in inputs]
    return pl.pallas_call(
        body,
        in_specs=specs,
        out_specs=outputs if outputs is not None else jax.tree.map(lambda _: vmem, shapes),
        out_shape=shapes,
        scratch_shapes=scratch,
        input_output_aliases=aliases or {},
        cost_estimate=pl.CostEstimate(flops=flops, bytes_accessed=moved, transcendentals=0),
        compiler_params=pltpu.CompilerParams(vmem_limit_bytes=GRANT),
    )


def place_kernel(where, received, onehot, out):
    picked = lax.dot_general(received[...], onehot[...], TRANSPOSED, preferred_element_type=jnp.float32)
    out[...] = picked.astype(jnp.bfloat16)


def place(where, received, onehot):
    shape = jax.ShapeDtypeStruct((COLS, ROWS), jnp.bfloat16)
    return call(place_kernel, [None] * 2, shape, 2 * ROWS * ROWS * COLS, ROWS * ROWS * 3)(where, received, onehot)


def fetch(where, w, pieces, rows, sems):
    copies = []
    for i, (_, _, shift, far) in enumerate(pieces):
        owner = far * NEAR + lax.rem(where[0] + shift, NEAR)
        source = w.at[pl.ds(pl.multiple_of(owner * COLS, COLS), COLS), :]
        copies.append(pltpu.make_async_copy(source, rows.at[i], sems.at[i]))
        copies[-1].start()
    return copies


def gradient(where, w, pieces, rows, sems, total):
    copies = fetch(where, w, pieces, rows, sems)
    for i, (ref, at, _, _) in enumerate(pieces):
        copies[i].wait()
        term = lax.dot_general(ref[at : at + COLS, :], rows[i], TRANSPOSED, preferred_element_type=jnp.float32)
        total = term if total is None else total + term
    return total


def w_scratch(count):
    return [pltpu.VMEM((count, COLS, FEAT), jnp.bfloat16), pltpu.SemaphoreType.DMA((count,))]


def grad_kernel(where, own, behind, ahead, far_a, far_b, w, x, gain, out, products, rows, sems):
    pieces = [
        (ref, COLS * far, shift, far)
        for ref, shift in ((own, 0), (behind, NEAR - 1), (ahead, 1))
        for far in range(FAR)
    ]
    pieces += [(ref, COLS * (far % 2), 2, far) for far, ref in enumerate((far_a, far_a, far_b, far_b))]
    total = gradient(where, w, pieces, rows, sems, None)
    out[...] = total
    part = x[...].astype(jnp.float32) * gain[...].astype(jnp.float32) * total
    lanes = part[:, :COLS]
    for i in range(1, FEAT // COLS):
        lanes = lanes + part[:, COLS * i : COLS * (i + 1)]
    products[...] = jnp.sum(lanes.T, axis=0, keepdims=True)


def grad_step(where, own, behind, ahead, far_a, far_b, w_kv, x, gain):
    shapes = [jax.ShapeDtypeStruct((ROWS, FEAT), jnp.float32), jax.ShapeDtypeStruct((1, ROWS), jnp.float32)]
    flops = 2 * TP * ROWS * FEAT * COLS
    hbm = pl.BlockSpec(memory_space=pltpu.HBM)
    return call(
        grad_kernel, [None] * 5 + [hbm, None, None], shapes, flops, 24 * ROWS * FEAT, scratch=w_scratch(TP)
    )(where, own, behind, ahead, far_a, far_b, w_kv, x, gain)


def split_rows(where, term):
    first = where[1] == 0
    low = jnp.concatenate([term[0:32], term[64:96]], axis=0)
    high = jnp.concatenate([term[32:64], term[96:128]], axis=0)
    return jnp.where(first, low, high), jnp.where(first, high, low).astype(jnp.bfloat16)


def weight_near_kernel(where, own, behind, ahead, normed, keep, send):
    for group, ref in enumerate((own, behind, ahead)):
        for far in range(FAR):
            term = jnp.dot(ref[COLS * far : COLS * (far + 1), :], normed[...], preferred_element_type=jnp.float32)
            kept, sent = split_rows(where, term)
            keep[far, group] = kept
            send[far, group] = sent


def weight_near(where, own, behind, ahead, normed):
    shapes = [jax.ShapeDtypeStruct((FAR, 3, COLS // 2, FEAT), kind) for kind in (jnp.float32, jnp.bfloat16)]
    flops = 6 * FAR * ROWS * FEAT * COLS
    return call(weight_near_kernel, [None] * 4, shapes, flops, 18 * ROWS * FEAT)(where, own, behind, ahead, normed)


def weight_far_kernel(where, far_a, far_b, normed, keep, send):
    for far in range(FAR):
        ref, at = (far_a, far_b)[far // 2], COLS * (far % 2)
        term = jnp.dot(ref[at : at + COLS, :], normed[...], preferred_element_type=jnp.float32)
        kept, sent = split_rows(where, term)
        keep[far] = kept
        send[far] = sent


def weight_far(where, far_a, far_b, normed):
    shapes = [jax.ShapeDtypeStruct((FAR, COLS // 2, FEAT), kind) for kind in (jnp.float32, jnp.bfloat16)]
    flops = 2 * FAR * ROWS * FEAT * COLS
    return call(weight_far_kernel, [None] * 3, shapes, flops, 8 * ROWS * FEAT)(where, far_a, far_b, normed)


def combine_near_kernel(where, keep, taken, out, total, sems):
    copies = []
    for far in range(FAR):
        for group, shift in enumerate((0, NEAR - 1, 1)):
            total[far, group] = (keep[far, group] + taken[far, group].astype(jnp.float32)).astype(jnp.bfloat16)
            to = out.at[far, lax.rem(where[0] + shift, NEAR)]
            copies.append(pltpu.make_async_copy(total.at[far, group], to, sems.at[far, group]))
            copies[-1].start()
    for copy in copies:
        copy.wait()


def combine_near(where, keep, taken):
    return call(
        combine_near_kernel,
        [None] * 2,
        jax.ShapeDtypeStruct((FAR, NEAR, COLS // 2, FEAT), jnp.bfloat16),
        3 * FAR * COLS * FEAT,
        12 * ROWS * FEAT,
        outputs=pl.BlockSpec(memory_space=pltpu.HBM),
        scratch=[pltpu.VMEM((FAR, 3, COLS // 2, FEAT), jnp.bfloat16), pltpu.SemaphoreType.DMA((FAR, 3))],
    )(where, keep, taken)


def combine_far_kernel(where, keep, taken, placed, out, total, sems):
    copies = []
    for far in range(FAR):
        total[far] = (keep[far] + taken[far].astype(jnp.float32)).astype(jnp.bfloat16)
        to = out.at[far, lax.rem(where[0] + 2, NEAR)]
        copies.append(pltpu.make_async_copy(total.at[far], to, sems.at[far]))
        copies[-1].start()
    for copy in copies:
        copy.wait()


def combine_far(where, keep, taken, placed):
    hbm = pl.BlockSpec(memory_space=pltpu.HBM)
    return call(
        combine_far_kernel,
        [None, None, hbm],
        jax.ShapeDtypeStruct(placed.shape, placed.dtype),
        FAR * COLS * FEAT,
        5 * ROWS * FEAT,
        outputs=hbm,
        scratch=[pltpu.VMEM((FAR, COLS // 2, FEAT), jnp.bfloat16), pltpu.SemaphoreType.DMA((FAR,))],
        aliases={3: 0},
    )(where, keep, taken, placed)


def tensor_sum(vector):
    spread = jnp.broadcast_to(vector.reshape(1, ROWS), (TP, ROWS))
    return jnp.sum(lax.all_to_all(spread, Z, split_axis=0, concat_axis=0, tiled=True), axis=0)


def hop(array, step):
    return lax.ppermute(array, Z, [(i, (i + step) % TP) for i in range(TP)])


def swap(array):
    return lax.ppermute(array, "core", [(0, 1), (1, 0)])


def gather_sum(vector):
    near = jnp.sum(lax.all_gather(vector, "zl", axis=0, tiled=True), axis=0, keepdims=True)
    return jnp.sum(lax.all_gather(near, "zh", axis=0, tiled=True), axis=0)


def step(layer_input, gain, w_kv, d_kv, destination):
    w_kv = pltpu.with_memory_space_constraint(w_kv, pltpu.HBM)
    where = jnp.stack([lax.axis_index("zl"), lax.axis_index("core")]).astype(jnp.int32)
    received = lax.all_to_all(d_kv, ("chip", "core"), split_axis=0, concat_axis=0, tiled=True)

    ids = jnp.arange(ROWS, dtype=jnp.int32)
    same = (destination[:, None] == destination[None, :]) & (ids[:, None] < ids[None, :])
    slot_rank = jnp.sum(same.astype(jnp.int32), axis=0)
    position = jnp.where(destination >= 0, destination * 8 + slot_rank, -1)
    onehot = (ids[:, None] == position[None, :]).astype(jnp.bfloat16)

    values = layer_input.astype(jnp.float32)
    gain_wide = gain.astype(jnp.float32)
    squares = jnp.sum(values * values, axis=1)
    onehot, squares, where = lax.optimization_barrier((onehot, squares, where))

    block = place(where, received, onehot)
    own = lax.all_gather(block, "zh", axis=0, tiled=True)
    own, squares = lax.optimization_barrier((own, squares))
    behind = hop(own, 1)
    ahead = hop(own, -1)
    inverse = lax.rsqrt(tensor_sum(squares) / D + EPS)
    normed = (values * inverse[:, None] * gain_wide).astype(jnp.bfloat16)
    far_a = hop(behind[:HALF], 1)
    far_b = hop(ahead[HALF:], -1)

    keep_near, send_near = weight_near(where, own, behind, ahead, normed)
    taken_near = swap(send_near)
    placed = combine_near(where, keep_near, taken_near)
    keep_far, send_far = weight_far(where, far_a, far_b, normed)
    taken_far = swap(send_far)
    pair = combine_far(where, keep_far, taken_far, placed)
    pair, x, inverse = lax.optimization_barrier((pair, layer_input, inverse))
    parts = lax.all_to_all(pair.reshape(CHIPS, 32, FEAT), "chip", split_axis=0, concat_axis=0, tiled=True)
    grad_weight = jnp.sum(parts.astype(jnp.float32), axis=0)

    dnormed, products = grad_step(where, own, behind, ahead, far_a, far_b, w_kv, x, gain[None, :])
    mean_dot = gather_sum(products) / D
    along = x.astype(jnp.float32) * (inverse**3 * mean_dot)[:, None]
    grad_x = (inverse[:, None] * gain_wide * dnormed - along).astype(jnp.bfloat16)
    return (grad_x, grad_weight)


def solution(mesh):
    fine = Mesh(mesh.devices.reshape(CHIPS, 2, FAR, NEAR), ("chip", "core", "zh", "zl"))
    dp = ("chip", "core")
    return jax.shard_map(
        step,
        mesh=fine,
        in_specs=(P(dp, Z), P(Z), P(None, Z), P(dp, Z), P(dp)),
        out_specs=(P(dp, Z), P(dp, Z)),
        check_vma=False,
    )
```

```python
import jax
import jax.numpy as jnp
from jax import lax
from jax.experimental import pallas as pl
from jax.experimental.pallas import tpu as pltpu
from jax.sharding import Mesh, PartitionSpec as P


D = 8192
EPS = 1e-06
ROWS = 512
FEAT = 512
COLS = 128
FAR = 4
NEAR = 4
TP = FAR * NEAR
CHIPS = 32
HALF = FAR * COLS // 2
GRANT = 24 * 1024 * 1024
Z = ("zh", "zl")
TRANSPOSED = (((0,), (0,)), ((), ()))


def call(body, inputs, shapes, flops, moved, outputs=None, scratch=(), aliases=None):
    vmem = pl.BlockSpec(memory_space=pltpu.VMEM)
    specs = [pl.BlockSpec(memory_space=pltpu.SMEM)] + [vmem if s is None else s for s in inputs]
    return pl.pallas_call(
        body,
        in_specs=specs,
        out_specs=outputs if outputs is not None else jax.tree.map(lambda _: vmem, shapes),
        out_shape=shapes,
        scratch_shapes=scratch,
        input_output_aliases=aliases or {},
        cost_estimate=pl.CostEstimate(flops=flops, bytes_accessed=moved, transcendentals=0),
        compiler_params=pltpu.CompilerParams(vmem_limit_bytes=GRANT),
    )


def place_kernel(where, received, onehot, out):
    picked = lax.dot_general(received[...], onehot[...], TRANSPOSED, preferred_element_type=jnp.float32)
    out[...] = picked.astype(jnp.bfloat16)


def place(where, received, onehot):
    shape = jax.ShapeDtypeStruct((COLS, ROWS), jnp.bfloat16)
    return call(place_kernel, [None] * 2, shape, 2 * ROWS * ROWS * COLS, ROWS * ROWS * 3)(where, received, onehot)


def fetch(where, w, pieces, rows, sems):
    copies = []
    for i, (_, _, shift, far) in enumerate(pieces):
        owner = far * NEAR + lax.rem(where[0] + shift, NEAR)
        source = w.at[pl.ds(pl.multiple_of(owner * COLS, COLS), COLS), :]
        copies.append(pltpu.make_async_copy(source, rows.at[i], sems.at[i]))
        copies[-1].start()
    return copies


def gradient(where, w, pieces, rows, sems, total):
    copies = fetch(where, w, pieces, rows, sems)
    for i, (ref, at, _, _) in enumerate(pieces):
        copies[i].wait()
        term = lax.dot_general(ref[at : at + COLS, :], rows[i], TRANSPOSED, preferred_element_type=jnp.float32)
        total = term if total is None else total + term
    return total


def w_scratch(count):
    return [pltpu.VMEM((count, COLS, FEAT), jnp.bfloat16), pltpu.SemaphoreType.DMA((count,))]


def grad_own_kernel(where, own, w, out, rows, sems):
    pieces = [(own, COLS * far, 0, far) for far in range(FAR)]
    out[...] = gradient(where, w, pieces, rows, sems, None)


def grad_own(where, own, w_kv):
    shape = jax.ShapeDtypeStruct((ROWS, FEAT), jnp.float32)
    flops = 2 * FAR * ROWS * FEAT * COLS
    hbm = pl.BlockSpec(memory_space=pltpu.HBM)
    return call(grad_own_kernel, [None, hbm], shape, flops, 8 * ROWS * FEAT, scratch=w_scratch(FAR))(where, own, w_kv)


def grad_rest_kernel(where, behind, ahead, far_a, far_b, w, before, x, gain, out, products, rows, sems):
    pieces = [(ref, COLS * far, shift, far) for ref, shift in ((behind, NEAR - 1), (ahead, 1)) for far in range(FAR)]
    pieces += [(ref, COLS * (far % 2), 2, far) for far, ref in enumerate((far_a, far_a, far_b, far_b))]
    total = gradient(where, w, pieces, rows, sems, before[...])
    out[...] = total
    part = x[...].astype(jnp.float32) * gain[...].astype(jnp.float32) * total
    lanes = part[:, :COLS]
    for i in range(1, FEAT // COLS):
        lanes = lanes + part[:, COLS * i : COLS * (i + 1)]
    products[...] = jnp.sum(lanes.T, axis=0, keepdims=True)


def grad_rest(where, behind, ahead, far_a, far_b, w_kv, before, x, gain):
    shapes = [jax.ShapeDtypeStruct((ROWS, FEAT), jnp.float32), jax.ShapeDtypeStruct((1, ROWS), jnp.float32)]
    flops = 6 * FAR * ROWS * FEAT * COLS
    hbm = pl.BlockSpec(memory_space=pltpu.HBM)
    return call(
        grad_rest_kernel,
        [None] * 4 + [hbm, None, None, None],
        shapes,
        flops,
        24 * ROWS * FEAT,
        scratch=w_scratch(3 * FAR),
        aliases={6: 0},
    )(where, behind, ahead, far_a, far_b, w_kv, before, x, gain)


def split_rows(where, term):
    first = where[1] == 0
    low = jnp.concatenate([term[0:32], term[64:96]], axis=0)
    high = jnp.concatenate([term[32:64], term[96:128]], axis=0)
    return jnp.where(first, low, high), jnp.where(first, high, low).astype(jnp.bfloat16)


def weight_near_kernel(where, own, behind, ahead, normed, keep, send):
    for group, ref in enumerate((own, behind, ahead)):
        for far in range(FAR):
            term = jnp.dot(ref[COLS * far : COLS * (far + 1), :], normed[...], preferred_element_type=jnp.float32)
            kept, sent = split_rows(where, term)
            keep[far, group] = kept
            send[far, group] = sent


def weight_near(where, own, behind, ahead, normed):
    shapes = [jax.ShapeDtypeStruct((FAR, 3, COLS // 2, FEAT), kind) for kind in (jnp.float32, jnp.bfloat16)]
    flops = 6 * FAR * ROWS * FEAT * COLS
    return call(weight_near_kernel, [None] * 4, shapes, flops, 18 * ROWS * FEAT)(where, own, behind, ahead, normed)


def weight_far_kernel(where, far_a, far_b, normed, keep, send):
    for far in range(FAR):
        ref, at = (far_a, far_b)[far // 2], COLS * (far % 2)
        term = jnp.dot(ref[at : at + COLS, :], normed[...], preferred_element_type=jnp.float32)
        kept, sent = split_rows(where, term)
        keep[far] = kept
        send[far] = sent


def weight_far(where, far_a, far_b, normed):
    shapes = [jax.ShapeDtypeStruct((FAR, COLS // 2, FEAT), kind) for kind in (jnp.float32, jnp.bfloat16)]
    flops = 2 * FAR * ROWS * FEAT * COLS
    return call(weight_far_kernel, [None] * 3, shapes, flops, 8 * ROWS * FEAT)(where, far_a, far_b, normed)


def combine_near_kernel(where, keep, taken, out, total, sems):
    copies = []
    for far in range(FAR):
        for group, shift in enumerate((0, NEAR - 1, 1)):
            total[far, group] = (keep[far, group] + taken[far, group].astype(jnp.float32)).astype(jnp.bfloat16)
            to = out.at[far, lax.rem(where[0] + shift, NEAR)]
            copies.append(pltpu.make_async_copy(total.at[far, group], to, sems.at[far, group]))
            copies[-1].start()
    for copy in copies:
        copy.wait()


def combine_near(where, keep, taken):
    return call(
        combine_near_kernel,
        [None] * 2,
        jax.ShapeDtypeStruct((FAR, NEAR, COLS // 2, FEAT), jnp.bfloat16),
        3 * FAR * COLS * FEAT,
        12 * ROWS * FEAT,
        outputs=pl.BlockSpec(memory_space=pltpu.HBM),
        scratch=[pltpu.VMEM((FAR, 3, COLS // 2, FEAT), jnp.bfloat16), pltpu.SemaphoreType.DMA((FAR, 3))],
    )(where, keep, taken)


def combine_far_kernel(where, keep, taken, placed, out, total, sems):
    copies = []
    for far in range(FAR):
        total[far] = (keep[far] + taken[far].astype(jnp.float32)).astype(jnp.bfloat16)
        to = out.at[far, lax.rem(where[0] + 2, NEAR)]
        copies.append(pltpu.make_async_copy(total.at[far], to, sems.at[far]))
        copies[-1].start()
    for copy in copies:
        copy.wait()


def combine_far(where, keep, taken, placed):
    hbm = pl.BlockSpec(memory_space=pltpu.HBM)
    return call(
        combine_far_kernel,
        [None, None, hbm],
        jax.ShapeDtypeStruct(placed.shape, placed.dtype),
        FAR * COLS * FEAT,
        5 * ROWS * FEAT,
        outputs=hbm,
        scratch=[pltpu.VMEM((FAR, COLS // 2, FEAT), jnp.bfloat16), pltpu.SemaphoreType.DMA((FAR,))],
        aliases={3: 0},
    )(where, keep, taken, placed)


def tensor_sum(vector):
    spread = jnp.broadcast_to(vector.reshape(1, ROWS), (TP, ROWS))
    return jnp.sum(lax.all_to_all(spread, Z, split_axis=0, concat_axis=0, tiled=True), axis=0)


def hop(array, step):
    return lax.ppermute(array, Z, [(i, (i + step) % TP) for i in range(TP)])


def swap(array):
    return lax.ppermute(array, "core", [(0, 1), (1, 0)])


def gather_sum(vector):
    return jnp.sum(lax.all_gather(vector, Z, axis=0, tiled=True), axis=0)


def step(layer_input, gain, w_kv, d_kv, destination):
    w_kv = pltpu.with_memory_space_constraint(w_kv, pltpu.HBM)
    where = jnp.stack([lax.axis_index("zl"), lax.axis_index("core")]).astype(jnp.int32)
    received = lax.all_to_all(d_kv, ("chip", "core"), split_axis=0, concat_axis=0, tiled=True)

    ids = jnp.arange(ROWS, dtype=jnp.int32)
    same = (destination[:, None] == destination[None, :]) & (ids[:, None] < ids[None, :])
    slot_rank = jnp.sum(same.astype(jnp.int32), axis=0)
    position = jnp.where(destination >= 0, destination * 8 + slot_rank, -1)
    onehot = (ids[:, None] == position[None, :]).astype(jnp.bfloat16)

    values = layer_input.astype(jnp.float32)
    gain_wide = gain.astype(jnp.float32)
    squares = jnp.sum(values * values, axis=1)
    onehot, squares, where = lax.optimization_barrier((onehot, squares, where))

    block = place(where, received, onehot)
    own = lax.all_gather(block, "zh", axis=0, tiled=True)
    own, squares = lax.optimization_barrier((own, squares))
    behind = hop(own, 1)
    ahead = hop(own, -1)
    inverse = lax.rsqrt(tensor_sum(squares) / D + EPS)
    normed = (values * inverse[:, None] * gain_wide).astype(jnp.bfloat16)
    far_a = hop(behind[:HALF], 1)
    far_b = hop(ahead[HALF:], -1)

    keep_near, send_near = weight_near(where, own, behind, ahead, normed)
    taken_near = swap(send_near)
    grad = grad_own(where, own, w_kv)
    placed = combine_near(where, keep_near, taken_near)
    keep_far, send_far = weight_far(where, far_a, far_b, normed)
    taken_far = swap(send_far)
    pair = combine_far(where, keep_far, taken_far, placed)
    pair, x, inverse = lax.optimization_barrier((pair, layer_input, inverse))
    parts = lax.all_to_all(pair.reshape(CHIPS, 32, FEAT), "chip", split_axis=0, concat_axis=0, tiled=True)
    grad_weight = jnp.sum(parts.astype(jnp.float32), axis=0)

    dnormed, products = grad_rest(where, behind, ahead, far_a, far_b, w_kv, grad, x, gain[None, :])
    mean_dot = gather_sum(products) / D
    along = x.astype(jnp.float32) * (inverse**3 * mean_dot)[:, None]
    grad_x = (inverse[:, None] * gain_wide * dnormed - along).astype(jnp.bfloat16)
    return (grad_x, grad_weight)


def solution(mesh):
    fine = Mesh(mesh.devices.reshape(CHIPS, 2, FAR, NEAR), ("chip", "core", "zh", "zl"))
    dp = ("chip", "core")
    return jax.shard_map(
        step,
        mesh=fine,
        in_specs=(P(dp, Z), P(Z), P(None, Z), P(dp, Z), P(dp)),
        out_specs=(P(dp, Z), P(dp, Z)),
        check_vma=False,
    )
```

```python
import jax
import jax.numpy as jnp
from jax import lax
from jax.experimental import pallas as pl
from jax.experimental.pallas import tpu as pltpu
from jax.sharding import Mesh, PartitionSpec as P


D = 8192
EPS = 1e-06
ROWS = 512
FEAT = 512
COLS = 128
FAR = 4
NEAR = 4
TP = FAR * NEAR
CHIPS = 32
GRANT = 24 * 1024 * 1024
Z = ("zh", "zl")
TRANSPOSED = (((0,), (0,)), ((), ()))


def call(body, inputs, shapes, flops, moved, outputs=None, scratch=(), aliases=None):
    vmem = pl.BlockSpec(memory_space=pltpu.VMEM)
    specs = [pl.BlockSpec(memory_space=pltpu.SMEM)] + [vmem if s is None else s for s in inputs]
    return pl.pallas_call(
        body,
        in_specs=specs,
        out_specs=outputs if outputs is not None else jax.tree.map(lambda _: vmem, shapes),
        out_shape=shapes,
        scratch_shapes=scratch,
        input_output_aliases=aliases or {},
        cost_estimate=pl.CostEstimate(flops=flops, bytes_accessed=moved, transcendentals=0),
        compiler_params=pltpu.CompilerParams(vmem_limit_bytes=GRANT),
    )


def place_kernel(where, received, onehot, out):
    picked = lax.dot_general(received[...], onehot[...], TRANSPOSED, preferred_element_type=jnp.float32)
    out[...] = picked.astype(jnp.bfloat16)


def place(where, received, onehot):
    shape = jax.ShapeDtypeStruct((COLS, ROWS), jnp.bfloat16)
    return call(place_kernel, [None] * 2, shape, 2 * ROWS * ROWS * COLS, ROWS * ROWS * 3)(where, received, onehot)


def gradient(where, w, groups, rows, sems, total):
    copies = []
    for group, (_, shift) in enumerate(groups):
        for far in range(FAR):
            i = FAR * group + far
            owner = far * NEAR + lax.rem(where[0] + shift, NEAR)
            source = w.at[pl.ds(pl.multiple_of(owner * COLS, COLS), COLS), :]
            copies.append(pltpu.make_async_copy(source, rows.at[COLS * i : COLS * (i + 1), :], sems.at[i]))
            copies[-1].start()
    for group, (ref, _) in enumerate(groups):
        for far in range(FAR):
            copies[FAR * group + far].wait()
        piece = rows[FAR * COLS * group : FAR * COLS * (group + 1), :]
        term = lax.dot_general(ref[...], piece, TRANSPOSED, preferred_element_type=jnp.float32)
        total = term if total is None else total + term
    return total


def w_scratch(groups):
    count = FAR * groups
    return [pltpu.VMEM((count * COLS, FEAT), jnp.bfloat16), pltpu.SemaphoreType.DMA((count,))]


def grad_near_kernel(where, own, behind, ahead, w, out, rows, sems):
    out[...] = gradient(where, w, [(own, 0), (behind, NEAR - 1), (ahead, 1)], rows, sems, None)


def grad_near(where, own, behind, ahead, w_kv):
    shape = jax.ShapeDtypeStruct((ROWS, FEAT), jnp.float32)
    flops = 6 * FAR * ROWS * FEAT * COLS
    hbm = pl.BlockSpec(memory_space=pltpu.HBM)
    return call(
        grad_near_kernel, [None] * 3 + [hbm], shape, flops, 14 * ROWS * FEAT, scratch=w_scratch(3)
    )(where, own, behind, ahead, w_kv)


def grad_far_kernel(where, far, w, before, x, gain, out, products, rows, sems):
    total = gradient(where, w, [(far, 2)], rows, sems, before[...])
    out[...] = total
    part = x[...].astype(jnp.float32) * gain[...].astype(jnp.float32) * total
    lanes = part[:, :COLS]
    for i in range(1, FEAT // COLS):
        lanes = lanes + part[:, COLS * i : COLS * (i + 1)]
    products[...] = jnp.sum(lanes.T, axis=0, keepdims=True)


def grad_far(where, far, w_kv, before, x, gain):
    shapes = [jax.ShapeDtypeStruct((ROWS, FEAT), jnp.float32), jax.ShapeDtypeStruct((1, ROWS), jnp.float32)]
    flops = 2 * FAR * ROWS * FEAT * COLS
    hbm = pl.BlockSpec(memory_space=pltpu.HBM)
    return call(
        grad_far_kernel,
        [None, hbm, None, None, None],
        shapes,
        flops,
        14 * ROWS * FEAT,
        scratch=w_scratch(1),
        aliases={3: 0},
    )(where, far, w_kv, before, x, gain)


def split_rows(where, term):
    first = where[1] == 0
    low = jnp.concatenate([term[0:32], term[64:96]], axis=0)
    high = jnp.concatenate([term[32:64], term[96:128]], axis=0)
    return jnp.where(first, low, high), jnp.where(first, high, low).astype(jnp.bfloat16)


def weight_near_kernel(where, own, behind, ahead, normed, keep, send):
    for group, ref in enumerate((own, behind, ahead)):
        for far in range(FAR):
            term = jnp.dot(ref[COLS * far : COLS * (far + 1), :], normed[...], preferred_element_type=jnp.float32)
            kept, sent = split_rows(where, term)
            keep[far, group] = kept
            send[far, group] = sent


def weight_near(where, own, behind, ahead, normed):
    shapes = [jax.ShapeDtypeStruct((FAR, 3, COLS // 2, FEAT), kind) for kind in (jnp.float32, jnp.bfloat16)]
    flops = 6 * FAR * ROWS * FEAT * COLS
    return call(weight_near_kernel, [None] * 4, shapes, flops, 18 * ROWS * FEAT)(where, own, behind, ahead, normed)


def weight_far_kernel(where, blocks, normed, keep, send):
    for far in range(FAR):
        term = jnp.dot(blocks[COLS * far : COLS * (far + 1), :], normed[...], preferred_element_type=jnp.float32)
        kept, sent = split_rows(where, term)
        keep[far] = kept
        send[far] = sent


def weight_far(where, blocks, normed):
    shapes = [jax.ShapeDtypeStruct((FAR, COLS // 2, FEAT), kind) for kind in (jnp.float32, jnp.bfloat16)]
    flops = 2 * FAR * ROWS * FEAT * COLS
    return call(weight_far_kernel, [None] * 2, shapes, flops, 8 * ROWS * FEAT)(where, blocks, normed)


def combine_near_kernel(where, keep, taken, out, total, sems):
    copies = []
    for far in range(FAR):
        for group, shift in enumerate((0, NEAR - 1, 1)):
            total[far, group] = (keep[far, group] + taken[far, group].astype(jnp.float32)).astype(jnp.bfloat16)
            to = out.at[far, lax.rem(where[0] + shift, NEAR)]
            copies.append(pltpu.make_async_copy(total.at[far, group], to, sems.at[far, group]))
            copies[-1].start()
    for copy in copies:
        copy.wait()


def combine_near(where, keep, taken):
    return call(
        combine_near_kernel,
        [None] * 2,
        jax.ShapeDtypeStruct((FAR, NEAR, COLS // 2, FEAT), jnp.bfloat16),
        3 * FAR * COLS * FEAT,
        12 * ROWS * FEAT,
        outputs=pl.BlockSpec(memory_space=pltpu.HBM),
        scratch=[pltpu.VMEM((FAR, 3, COLS // 2, FEAT), jnp.bfloat16), pltpu.SemaphoreType.DMA((FAR, 3))],
    )(where, keep, taken)


def combine_far_kernel(where, keep, taken, placed, out, total, sems):
    copies = []
    for far in range(FAR):
        total[far] = (keep[far] + taken[far].astype(jnp.float32)).astype(jnp.bfloat16)
        to = out.at[far, lax.rem(where[0] + 2, NEAR)]
        copies.append(pltpu.make_async_copy(total.at[far], to, sems.at[far]))
        copies[-1].start()
    for copy in copies:
        copy.wait()


def combine_far(where, keep, taken, placed):
    hbm = pl.BlockSpec(memory_space=pltpu.HBM)
    return call(
        combine_far_kernel,
        [None, None, hbm],
        jax.ShapeDtypeStruct(placed.shape, placed.dtype),
        FAR * COLS * FEAT,
        5 * ROWS * FEAT,
        outputs=hbm,
        scratch=[pltpu.VMEM((FAR, COLS // 2, FEAT), jnp.bfloat16), pltpu.SemaphoreType.DMA((FAR,))],
        aliases={3: 0},
    )(where, keep, taken, placed)


def tensor_sum(vector):
    spread = jnp.broadcast_to(vector.reshape(1, ROWS), (TP, ROWS))
    return jnp.sum(lax.all_to_all(spread, Z, split_axis=0, concat_axis=0, tiled=True), axis=0)


def hop(array, step):
    return lax.ppermute(array, Z, [(i, (i + step) % TP) for i in range(TP)])


def swap(array):
    return lax.ppermute(array, "core", [(0, 1), (1, 0)])


def gather_sum(vector):
    return jnp.sum(lax.all_gather(vector, Z, axis=0, tiled=True), axis=0)


def step(layer_input, gain, w_kv, d_kv, destination):
    w_kv = pltpu.with_memory_space_constraint(w_kv, pltpu.HBM)
    where = jnp.stack([lax.axis_index("zl"), lax.axis_index("core")]).astype(jnp.int32)
    received = lax.all_to_all(d_kv, ("chip", "core"), split_axis=0, concat_axis=0, tiled=True)

    ids = jnp.arange(ROWS, dtype=jnp.int32)
    same = (destination[:, None] == destination[None, :]) & (ids[:, None] < ids[None, :])
    slot_rank = jnp.sum(same.astype(jnp.int32), axis=0)
    position = jnp.where(destination >= 0, destination * 8 + slot_rank, -1)
    onehot = (ids[:, None] == position[None, :]).astype(jnp.bfloat16)

    values = layer_input.astype(jnp.float32)
    gain_wide = gain.astype(jnp.float32)
    squares = jnp.sum(values * values, axis=1)
    onehot, squares, where = lax.optimization_barrier((onehot, squares, where))

    block = place(where, received, onehot)
    own = lax.all_gather(block, "zh", axis=0, tiled=True)
    own, squares = lax.optimization_barrier((own, squares))
    behind = hop(own, 1)
    ahead = hop(own, -1)
    inverse = lax.rsqrt(tensor_sum(squares) / D + EPS)
    normed = (values * inverse[:, None] * gain_wide).astype(jnp.bfloat16)
    far = hop(behind, 1)

    keep_near, send_near = weight_near(where, own, behind, ahead, normed)
    taken_near = swap(send_near)
    grad = grad_near(where, own, behind, ahead, w_kv)
    placed = combine_near(where, keep_near, taken_near)
    keep_far, send_far = weight_far(where, far, normed)
    taken_far = swap(send_far)
    pair = combine_far(where, keep_far, taken_far, placed)
    pair, x, inverse = lax.optimization_barrier((pair, layer_input, inverse))
    parts = lax.all_to_all(pair.reshape(CHIPS, 32, FEAT), "chip", split_axis=0, concat_axis=0, tiled=True)
    grad_weight = jnp.sum(parts.astype(jnp.float32), axis=0)

    dnormed, products = grad_far(where, far, w_kv, grad, x, gain[None, :])
    mean_dot = gather_sum(products) / D
    along = x.astype(jnp.float32) * (inverse**3 * mean_dot)[:, None]
    grad_x = (inverse[:, None] * gain_wide * dnormed - along).astype(jnp.bfloat16)
    return (grad_x, grad_weight)


def solution(mesh):
    fine = Mesh(mesh.devices.reshape(CHIPS, 2, FAR, NEAR), ("chip", "core", "zh", "zl"))
    dp = ("chip", "core")
    return jax.shard_map(
        step,
        mesh=fine,
        in_specs=(P(dp, Z), P(Z), P(None, Z), P(dp, Z), P(dp)),
        out_specs=(P(dp, Z), P(dp, Z)),
        check_vma=False,
    )
```

```python
import jax
import jax.numpy as jnp
from jax import lax
from jax.experimental import pallas as pl
from jax.experimental.pallas import tpu as pltpu
from jax.sharding import Mesh, PartitionSpec as P


D = 8192
EPS = 1e-06
ROWS = 512
FEAT = 512
COLS = 128
FAR = 4
NEAR = 4
TP = FAR * NEAR
CHIPS = 32
GRANT = 24 * 1024 * 1024
Z = ("zh", "zl")
TRANSPOSED = (((0,), (0,)), ((), ()))


def call(body, inputs, shapes, flops, moved, outputs=None, scratch=(), aliases=None):
    vmem = pl.BlockSpec(memory_space=pltpu.VMEM)
    specs = [pl.BlockSpec(memory_space=pltpu.SMEM)] + [vmem if s is None else s for s in inputs]
    return pl.pallas_call(
        body,
        in_specs=specs,
        out_specs=outputs if outputs is not None else jax.tree.map(lambda _: vmem, shapes),
        out_shape=shapes,
        scratch_shapes=scratch,
        input_output_aliases=aliases or {},
        cost_estimate=pl.CostEstimate(flops=flops, bytes_accessed=moved, transcendentals=0),
        compiler_params=pltpu.CompilerParams(vmem_limit_bytes=GRANT),
    )


def place_kernel(where, received, onehot, out):
    picked = lax.dot_general(received[...], onehot[...], TRANSPOSED, preferred_element_type=jnp.float32)
    out[...] = picked.astype(jnp.bfloat16)


def place(where, received, onehot):
    shape = jax.ShapeDtypeStruct((COLS, ROWS), jnp.bfloat16)
    return call(place_kernel, [None] * 2, shape, 2 * ROWS * ROWS * COLS, ROWS * ROWS * 3)(where, received, onehot)


def gradient(where, w, groups, rows, sems, total):
    copies = []
    for group, (_, shift) in enumerate(groups):
        for far in range(FAR):
            i = FAR * group + far
            owner = far * NEAR + lax.rem(where[0] + shift, NEAR)
            source = w.at[pl.ds(pl.multiple_of(owner * COLS, COLS), COLS), :]
            copies.append(pltpu.make_async_copy(source, rows.at[COLS * i : COLS * (i + 1), :], sems.at[i]))
            copies[-1].start()
    for group, (ref, _) in enumerate(groups):
        for far in range(FAR):
            copies[FAR * group + far].wait()
        piece = rows[FAR * COLS * group : FAR * COLS * (group + 1), :]
        term = lax.dot_general(ref[...], piece, TRANSPOSED, preferred_element_type=jnp.float32)
        total = term if total is None else total + term
    return total


def w_scratch(groups):
    count = FAR * groups
    return [pltpu.VMEM((count * COLS, FEAT), jnp.bfloat16), pltpu.SemaphoreType.DMA((count,))]


def grad_near_kernel(where, own, behind, ahead, w, out, rows, sems):
    out[...] = gradient(where, w, [(own, 0), (behind, NEAR - 1), (ahead, 1)], rows, sems, None)


def grad_near(where, own, behind, ahead, w_kv):
    shape = jax.ShapeDtypeStruct((ROWS, FEAT), jnp.float32)
    flops = 6 * FAR * ROWS * FEAT * COLS
    hbm = pl.BlockSpec(memory_space=pltpu.HBM)
    return call(
        grad_near_kernel, [None] * 3 + [hbm], shape, flops, 14 * ROWS * FEAT, scratch=w_scratch(3)
    )(where, own, behind, ahead, w_kv)


def grad_far_kernel(where, far, w, before, x, gain, out, products, rows, sems):
    total = gradient(where, w, [(far, 2)], rows, sems, before[...])
    out[...] = total
    part = x[...].astype(jnp.float32) * gain[...].astype(jnp.float32) * total
    lanes = part[:, :COLS]
    for i in range(1, FEAT // COLS):
        lanes = lanes + part[:, COLS * i : COLS * (i + 1)]
    products[...] = jnp.sum(lanes.T, axis=0, keepdims=True)


def grad_far(where, far, w_kv, before, x, gain):
    shapes = [jax.ShapeDtypeStruct((ROWS, FEAT), jnp.float32), jax.ShapeDtypeStruct((1, ROWS), jnp.float32)]
    flops = 2 * FAR * ROWS * FEAT * COLS
    hbm = pl.BlockSpec(memory_space=pltpu.HBM)
    return call(
        grad_far_kernel,
        [None, hbm, None, None, None],
        shapes,
        flops,
        14 * ROWS * FEAT,
        scratch=w_scratch(1),
        aliases={3: 0},
    )(where, far, w_kv, before, x, gain)


def split_rows(where, term):
    first = where[1] == 0
    low = jnp.concatenate([term[0:32], term[64:96]], axis=0)
    high = jnp.concatenate([term[32:64], term[96:128]], axis=0)
    return jnp.where(first, low, high), jnp.where(first, high, low).astype(jnp.bfloat16)


def weight_near_kernel(where, own, behind, ahead, normed, keep, send):
    for group, ref in enumerate((own, behind, ahead)):
        for far in range(FAR):
            term = jnp.dot(ref[COLS * far : COLS * (far + 1), :], normed[...], preferred_element_type=jnp.float32)
            kept, sent = split_rows(where, term)
            keep[far, group] = kept
            send[far, group] = sent


def weight_near(where, own, behind, ahead, normed):
    shapes = [jax.ShapeDtypeStruct((FAR, 3, COLS // 2, FEAT), kind) for kind in (jnp.float32, jnp.bfloat16)]
    flops = 6 * FAR * ROWS * FEAT * COLS
    return call(weight_near_kernel, [None] * 4, shapes, flops, 18 * ROWS * FEAT)(where, own, behind, ahead, normed)


def weight_far_kernel(where, blocks, normed, keep, send):
    for far in range(FAR):
        term = jnp.dot(blocks[COLS * far : COLS * (far + 1), :], normed[...], preferred_element_type=jnp.float32)
        kept, sent = split_rows(where, term)
        keep[far] = kept
        send[far] = sent


def weight_far(where, blocks, normed):
    shapes = [jax.ShapeDtypeStruct((FAR, COLS // 2, FEAT), kind) for kind in (jnp.float32, jnp.bfloat16)]
    flops = 2 * FAR * ROWS * FEAT * COLS
    return call(weight_far_kernel, [None] * 2, shapes, flops, 8 * ROWS * FEAT)(where, blocks, normed)


def combine_near_kernel(where, keep, taken, out, total, sems):
    copies = []
    for far in range(FAR):
        for group, shift in enumerate((0, NEAR - 1, 1)):
            total[far, group] = (keep[far, group] + taken[far, group].astype(jnp.float32)).astype(jnp.bfloat16)
            to = out.at[far, lax.rem(where[0] + shift, NEAR)]
            copies.append(pltpu.make_async_copy(total.at[far, group], to, sems.at[far, group]))
            copies[-1].start()
    for copy in copies:
        copy.wait()


def combine_near(where, keep, taken):
    return call(
        combine_near_kernel,
        [None] * 2,
        jax.ShapeDtypeStruct((FAR, NEAR, COLS // 2, FEAT), jnp.bfloat16),
        3 * FAR * COLS * FEAT,
        12 * ROWS * FEAT,
        outputs=pl.BlockSpec(memory_space=pltpu.HBM),
        scratch=[pltpu.VMEM((FAR, 3, COLS // 2, FEAT), jnp.bfloat16), pltpu.SemaphoreType.DMA((FAR, 3))],
    )(where, keep, taken)


def combine_far_kernel(where, keep, taken, placed, out, total, sems):
    copies = []
    for far in range(FAR):
        total[far] = (keep[far] + taken[far].astype(jnp.float32)).astype(jnp.bfloat16)
        to = out.at[far, lax.rem(where[0] + 2, NEAR)]
        copies.append(pltpu.make_async_copy(total.at[far], to, sems.at[far]))
        copies[-1].start()
    for copy in copies:
        copy.wait()


def combine_far(where, keep, taken, placed):
    hbm = pl.BlockSpec(memory_space=pltpu.HBM)
    return call(
        combine_far_kernel,
        [None, None, hbm],
        jax.ShapeDtypeStruct(placed.shape, placed.dtype),
        FAR * COLS * FEAT,
        5 * ROWS * FEAT,
        outputs=hbm,
        scratch=[pltpu.VMEM((FAR, COLS // 2, FEAT), jnp.bfloat16), pltpu.SemaphoreType.DMA((FAR,))],
        aliases={3: 0},
    )(where, keep, taken, placed)


def total_kernel(where, parts, out, buffer, sems):
    step = CHIPS // 4
    copies = []
    for i in range(4):
        piece = slice(step * i, step * (i + 1))
        copies.append(pltpu.make_async_copy(parts.at[piece], buffer.at[piece], sems.at[i]))
        copies[-1].start()
    total = jnp.zeros(out.shape, jnp.float32)
    for i in range(4):
        copies[i].wait()
        for j in range(step * i, step * (i + 1)):
            total = total + buffer[j].astype(jnp.float32)
    out[...] = total


def total(where, parts):
    return call(
        total_kernel,
        [pl.BlockSpec(memory_space=pltpu.HBM)],
        jax.ShapeDtypeStruct(parts.shape[1:], jnp.float32),
        parts.size,
        2 * parts.size,
        scratch=[pltpu.VMEM(parts.shape, parts.dtype), pltpu.SemaphoreType.DMA((4,))],
    )(where, parts)


def tensor_sum(vector):
    spread = jnp.broadcast_to(vector.reshape(1, ROWS), (TP, ROWS))
    return jnp.sum(lax.all_to_all(spread, Z, split_axis=0, concat_axis=0, tiled=True), axis=0)


def hop(array, step):
    return lax.ppermute(array, Z, [(i, (i + step) % TP) for i in range(TP)])


def swap(array):
    return lax.ppermute(array, "core", [(0, 1), (1, 0)])


def gather_sum(vector):
    return jnp.sum(lax.all_gather(vector, Z, axis=0, tiled=True), axis=0)


def step(layer_input, gain, w_kv, d_kv, destination):
    w_kv = pltpu.with_memory_space_constraint(w_kv, pltpu.HBM)
    where = jnp.stack([lax.axis_index("zl"), lax.axis_index("core")]).astype(jnp.int32)
    received = lax.all_to_all(d_kv, ("chip", "core"), split_axis=0, concat_axis=0, tiled=True)

    ids = jnp.arange(ROWS, dtype=jnp.int32)
    same = (destination[:, None] == destination[None, :]) & (ids[:, None] < ids[None, :])
    slot_rank = jnp.sum(same.astype(jnp.int32), axis=0)
    position = jnp.where(destination >= 0, destination * 8 + slot_rank, -1)
    onehot = (ids[:, None] == position[None, :]).astype(jnp.bfloat16)

    values = layer_input.astype(jnp.float32)
    gain_wide = gain.astype(jnp.float32)
    squares = jnp.sum(values * values, axis=1)
    onehot, squares, where = lax.optimization_barrier((onehot, squares, where))

    block = place(where, received, onehot)
    own = lax.all_gather(block, "zh", axis=0, tiled=True)
    own, squares = lax.optimization_barrier((own, squares))
    behind = hop(own, 1)
    ahead = hop(own, -1)
    inverse = lax.rsqrt(tensor_sum(squares) / D + EPS)
    normed = (values * inverse[:, None] * gain_wide).astype(jnp.bfloat16)
    far = hop(behind, 1)

    keep_near, send_near = weight_near(where, own, behind, ahead, normed)
    taken_near = swap(send_near)
    grad = grad_near(where, own, behind, ahead, w_kv)
    placed = combine_near(where, keep_near, taken_near)
    keep_far, send_far = weight_far(where, far, normed)
    taken_far = swap(send_far)
    pair = combine_far(where, keep_far, taken_far, placed)
    pair, x, inverse = lax.optimization_barrier((pair, layer_input, inverse))
    parts = lax.all_to_all(pair.reshape(CHIPS, 32, FEAT), "chip", split_axis=0, concat_axis=0, tiled=True)
    grad_weight = total(where, parts)

    dnormed, products = grad_far(where, far, w_kv, grad, x, gain[None, :])
    mean_dot = gather_sum(products) / D
    along = x.astype(jnp.float32) * (inverse**3 * mean_dot)[:, None]
    grad_x = (inverse[:, None] * gain_wide * dnormed - along).astype(jnp.bfloat16)
    return (grad_x, grad_weight)


def solution(mesh):
    fine = Mesh(mesh.devices.reshape(CHIPS, 2, FAR, NEAR), ("chip", "core", "zh", "zl"))
    dp = ("chip", "core")
    return jax.shard_map(
        step,
        mesh=fine,
        in_specs=(P(dp, Z), P(Z), P(None, Z), P(dp, Z), P(dp)),
        out_specs=(P(dp, Z), P(dp, Z)),
        check_vma=False,
    )
```
